256 devices in a mesh: row: 32 (over x_lo, z, core), col: 8 (over y, x_hi).
Axes of the slice: x: 4 (x_hi: 2, x_lo: 2; x = x_hi * 2 + x_lo), y: 4, z: 8, core: 2. Of those that a mesh axis runs over, the one named last changes fastest.
Arguments:
- covariance: float32 [16384, 16384], P('row', 'col'), may hold values from -6 to 6
- lon_courant: float32 [128, 128], replicated, may hold values from 0.05 to 0.95
- lat_courant: float32 [128, 128], replicated, may hold values from 0.05 to 0.9
- zonal_upwind_sign: int32 [128, 128], replicated, may hold values 0 or 1
- lat_sign: int32 [128, 128], replicated, may hold values 0 or 1
- cycle_counts: int32 [128], replicated, may hold values from 1 to 4
Outputs:
- forecast: float32 [16384, 16384], P('row', 'col')
The draws below stay inside these ranges and needn't reach their ends.
Inputs may be any that keep to these rules, and one draw needn't show every extreme that they name: `zonal_upwind_sign`: 1 where the wind blows toward growing longitude, 0 otherwise. `lat_sign`: 1 where the wind blows toward growing latitude, 0 otherwise.
All inputs are finite; a program needn't handle non-finite values.
Results may differ from the reference program's by a relative error of at most 0.00002.
Values sent between devices are 32-bit elements; how exact they have to be, the bound alone decides.
A program may use at most 128 MiB of HBM per device.

```python
import math
import jax
import jax.numpy as jnp
from jax import lax

NLAT = 128
NLON = 128
SUBCYCLES = 4
GRID_POINTS = 16384


def set_ends(entries, key, low, largest):
    longest = entries.shape.index(max(entries.shape))
    spots = []
    for shift in (0, 1):
        where = [jax.random.randint(jax.random.fold_in(key, axis), (), 0, length) for axis, length in enumerate(entries.shape)]
        where[longest] = (where[longest] + shift) % entries.shape[longest]
        spots.append(tuple(where))
    return entries.at[spots[0]].set(low).at[spots[1]].set(largest)


def shard_levels(own_key, extent, shards, least, largest):
    gain, own = 1.0, jax.random.fold_in(own_key, 6)
    for axis_at, parts in shards:
        draws = jnp.exp(jax.random.uniform(jax.random.fold_in(own, axis_at), (parts,), jnp.float32, least / len(shards), largest / len(shards)))
        gain = gain * jnp.repeat(draws, extent[axis_at] // parts).reshape([-1 if axis == axis_at else 1 for axis in range(len(extent))])
    return gain


def normal_values(stream_key, extent, scale, bound, pieces=(), kind=jnp.bfloat16):
    values = scale * jax.random.normal(stream_key, extent, jnp.float32)
    if pieces:
        values = values * shard_levels(stream_key, extent, pieces, -0.22, 0.18)
    return jnp.clip(values, -bound, bound).astype(kind)


def setup_inputs(seed: int = 0) -> dict:
    arg_keys = jax.random.split(jax.random.key(seed), 7)
    return {
        "covariance": normal_values(arg_keys[0], (GRID_POINTS, GRID_POINTS), 1.0, 6.0, ((0, 32), (1, 8)), jnp.float32),
        "lon_courant": jnp.clip(jnp.exp(jax.random.uniform(arg_keys[1], (NLAT, NLON), jnp.float32, math.log(0.05), math.log(0.95))), 0.05, 0.95),
        "lat_courant": jnp.clip(jnp.exp(jax.random.uniform(arg_keys[2], (NLAT, NLON), jnp.float32, math.log(0.05), math.log(0.9))), 0.05, 0.9),
        "zonal_upwind_sign": set_ends((jax.random.randint(arg_keys[3], (NLAT, NLON), 0, 2) < 1).astype(jnp.int32), jax.random.fold_in(arg_keys[3], 1), 0, 1),
        "lat_sign": set_ends((jax.random.randint(arg_keys[4], (NLAT, NLON), 0, 2) < 1).astype(jnp.int32), jax.random.fold_in(arg_keys[4], 1), 0, 1),
        "cycle_counts": set_ends(jax.random.randint(arg_keys[5], (NLAT,), 1, SUBCYCLES + 1), jax.random.fold_in(arg_keys[5], 1), 1, SUBCYCLES).astype(jnp.int32),
    }


def lat_step(values, courant, upwind_sign):
    zero_row = jnp.zeros_like(values[:1])
    below_cells = jnp.concatenate([zero_row, values[:-1]], axis=0)
    above_cells = jnp.concatenate([values[1:], zero_row], axis=0)
    nearby = jnp.where(upwind_sign == 1, below_cells, above_cells)
    return values - courant * (values - nearby)


def advance(values, lon_courant, lat_courant, zonal_upwind_sign, lat_sign, cycle_counts):
    lon_rate = lon_courant[:, :, None]
    lat_rate = lat_courant[:, :, None]
    zonal_heading = zonal_upwind_sign[:, :, None]
    lat_dir = lat_sign[:, :, None]
    counts = cycle_counts[:, None, None]
    values = lat_step(values, lat_rate, lat_dir)

    def subcycle(cycle_index, current):
        cell_rate = jnp.where(cycle_index < counts, lon_rate, jnp.zeros_like(lon_rate))
        western_neighbour = jnp.roll(current, 1, axis=1)
        east_cell = jnp.roll(current, -1, axis=1)
        nearby = jnp.where(zonal_heading == 1, western_neighbour, east_cell)
        return current - cell_rate * (current - nearby)

    values = lax.fori_loop(0, SUBCYCLES, subcycle, values)
    return lat_step(values, lat_rate, lat_dir)


def reference(covariance, lon_courant, lat_courant, zonal_upwind_sign, lat_sign, cycle_counts):
    block_count = 16
    block_width = GRID_POINTS // block_count

    def zonal_pass(block):
        return advance(block, lon_courant, lat_courant, zonal_upwind_sign, lat_sign, cycle_counts)

    col_blocks = covariance.reshape(NLAT, NLON, block_count, block_width).transpose(2, 0, 1, 3)
    advanced_blocks = lax.map(zonal_pass, col_blocks)
    advanced = advanced_blocks.transpose(1, 2, 0, 3).reshape(GRID_POINTS, GRID_POINTS)
    row_block_list = advanced.reshape(block_count, block_width, NLAT, NLON).transpose(0, 2, 3, 1)
    predicted_blocks = lax.map(zonal_pass, row_block_list)
    return predicted_blocks.transpose(0, 3, 1, 2).reshape(GRID_POINTS, GRID_POINTS)
```

```python
import functools

import jax
import jax.numpy as jnp
from jax import lax
from jax.experimental import pallas as pl
from jax.experimental.pallas import tpu as pltpu
from jax.sharding import PartitionSpec as P

MESH = pl.DeviceIdType.MESH
NLAT = 128
NLON = 128
SUBCYCLES = 4
WIDE = 256
F32 = jnp.float32
BF16 = jnp.bfloat16


def split(values):
    high = values.astype(BF16)
    return high, (values - high.astype(F32)).astype(BF16)


def dot(a, b):
    return jnp.dot(a, b, preferred_element_type=F32)


def upwind(center, below, above, courant, from_below):
    nearby = jnp.where(from_below, below, above)
    return center - courant * (center - nearby)


def sweep_matrix(lat, lon_ref, zonal_ref, counts_ref):
    rate = lon_ref[pl.ds(lat, 1), :]
    west = jnp.broadcast_to(zonal_ref[pl.ds(lat, 1), :], (NLON, NLON)) == 1
    count = counts_ref[lat]
    row = lax.broadcasted_iota(jnp.int32, (NLON, NLON), 0)
    column = lax.broadcasted_iota(jnp.int32, (NLON, NLON), 1)
    current = jnp.where(row == column, 1.0, 0.0).astype(F32)
    for cycle in range(SUBCYCLES):
        cell_rate = jnp.where(cycle < count, rate, 0.0)
        nearby = jnp.where(
            west, pltpu.roll(current, 1, 1), pltpu.roll(current, NLON - 1, 1)
        )
        current = current - cell_rate * (current - nearby)
    return current


def kernel(
    rows_n, cols_n,
    cov, lon_ref, lat_ref, zonal_ref, sign_ref, counts_ref,
    out,
    ext, wide, row_mid, col_mid, final,
    row_rate, row_sign, row_hi, row_lo, col_hi, col_lo,
    load_sem, row_send, row_recv, col_send, col_recv, out_sem,
):
    r, c = lax.axis_index("row"), lax.axis_index("col")
    rows, cols = cov.shape
    row_lats, col_lats = rows // NLON, cols // NLON
    chunks = cols // WIDE
    halo = 2 * NLON
    first_row, first_col = r * row_lats, c * col_lats
    has_down, has_up = r > 0, r < rows_n - 1
    has_left, has_right = c > 0, c < cols_n - 1
    down, up = (r - 1, c), (r + 1, c)
    left, right = (r, c - 1), (r, c + 1)

    barrier = pltpu.get_barrier_semaphore()
    for exists, device in ((has_down, down), (has_up, up), (has_left, left), (has_right, right)):
        @pl.when(exists)
        def _():
            pl.semaphore_signal(barrier, inc=1, device_id=device, device_id_type=MESH)

    load = pltpu.make_async_copy(cov, ext.at[pl.ds(halo, rows), :], load_sem)
    load.start()

    pl.semaphore_wait(
        barrier,
        has_down.astype(jnp.int32) + has_up.astype(jnp.int32)
        + has_left.astype(jnp.int32) + has_right.astype(jnp.int32),
    )

    def chunk_columns(chunk):
        return pl.ds(pl.multiple_of(chunk * WIDE, WIDE), WIDE)

    def to_down(chunk):
        return pltpu.make_async_remote_copy(
            cov.at[pl.ds(0, halo), chunk_columns(chunk)],
            ext.at[pl.ds(halo + rows, halo), chunk_columns(chunk)],
            row_send.at[0, chunk], row_recv.at[0, chunk],
            device_id=down, device_id_type=MESH,
        )

    def to_up(chunk):
        return pltpu.make_async_remote_copy(
            cov.at[pl.ds(rows - halo, halo), chunk_columns(chunk)],
            ext.at[pl.ds(0, halo), chunk_columns(chunk)],
            row_send.at[1, chunk], row_recv.at[1, chunk],
            device_id=up, device_id_type=MESH,
        )

    order = [0, chunks - 1, *range(1, chunks - 1)]

    @pl.when(has_down)
    def _():
        for chunk in order:
            to_down(chunk).start()

    @pl.when(has_up)
    def _():
        for chunk in order:
            to_up(chunk).start()

    @pl.when(jnp.logical_not(has_down))
    def _():
        ext[pl.ds(0, halo), :] = jnp.zeros((halo, cols), F32)

    @pl.when(jnp.logical_not(has_up))
    def _():
        ext[pl.ds(halo + rows, halo), :] = jnp.zeros((halo, cols), F32)

    @pl.when(jnp.logical_not(has_left))
    def _():
        wide[:, pl.ds(0, halo)] = jnp.zeros((rows, halo), F32)

    @pl.when(jnp.logical_not(has_right))
    def _():
        wide[:, pl.ds(halo + cols, halo)] = jnp.zeros((rows, halo), F32)

    def clamped(lat):
        return jnp.clip(lat, 0, NLAT - 1)

    def courant_of(lat):
        inside = jnp.logical_and(lat >= 0, lat < NLAT)
        return jnp.where(inside, lat_ref[pl.ds(clamped(lat), 1), :], 0.0)

    def prepare_row(i, carry):
        lat = first_row - 1 + i
        at = clamped(lat)
        row_rate[i] = jnp.broadcast_to(courant_of(lat), (NLON, NLON)).T
        row_sign[i] = jnp.broadcast_to(
            sign_ref[pl.ds(at, 1), :].astype(F32), (NLON, NLON)
        ).T
        high, low = split(sweep_matrix(at, lon_ref, zonal_ref, counts_ref).T)
        row_hi[i] = high
        row_lo[i] = low
        return carry

    lax.fori_loop(0, row_lats + 2, prepare_row, 0)

    def prepare_col(i, carry):
        at = clamped(first_col - 1 + i)
        high, low = split(sweep_matrix(at, lon_ref, zonal_ref, counts_ref))
        col_hi[i] = high
        col_lo[i] = low
        return carry

    def both(table):
        return jnp.concatenate([table, table], axis=1)

    def row_chunk(chunk):
        @pl.when(has_down)
        def _():
            to_up(chunk).wait_recv()

        @pl.when(has_up)
        def _():
            to_down(chunk).wait_recv()

        at = chunk_columns(chunk)
        for i in range(row_lats + 2):
            below = ext[pl.ds(i * NLON, NLON), at]
            center = ext[pl.ds((i + 1) * NLON, NLON), at]
            above = ext[pl.ds((i + 2) * NLON, NLON), at]
            moved = upwind(center, below, above, both(row_rate[i]), both(row_sign[i]) == 1.0)
            high, low = split(moved)
            row_mid[i] = (
                dot(row_hi[i], high) + (dot(row_hi[i], low) + dot(row_lo[i], high))
            )
        own = pl.ds(pl.multiple_of(halo + chunk * WIDE, WIDE), WIDE)
        for i in range(1, row_lats + 1):
            wide[pl.ds((i - 1) * NLON, NLON), own] = upwind(
                row_mid[i], row_mid[i - 1], row_mid[i + 1],
                both(row_rate[i]), both(row_sign[i]) == 1.0,
            )

    def lat_columns(index):
        return pl.ds(pl.multiple_of(index * NLON, NLON), NLON)

    def col_middle(i):
        lat = first_col - 1 + i
        from_below = sign_ref[pl.ds(clamped(lat), 1), :] == 1
        moved = upwind(
            wide[:, lat_columns(i + 1)], wide[:, lat_columns(i)], wide[:, lat_columns(i + 2)],
            courant_of(lat), from_below,
        )
        high, low = split(moved)
        col_mid[:, lat_columns(i)] = (
            dot(high, col_hi[i]) + (dot(low, col_hi[i]) + dot(high, col_lo[i]))
        )

    def col_final(k):
        lat = first_col + k
        from_below = sign_ref[pl.ds(lat, 1), :] == 1
        final[:, lat_columns(k)] = upwind(
            col_mid[:, lat_columns(k + 1)], col_mid[:, lat_columns(k)],
            col_mid[:, lat_columns(k + 2)], courant_of(lat), from_below,
        )

    def to_left():
        return pltpu.make_async_remote_copy(
            wide.at[:, pl.ds(halo, halo)], wide.at[:, pl.ds(halo + cols, halo)],
            col_send.at[0], col_recv.at[0], device_id=left, device_id_type=MESH,
        )

    def to_right():
        return pltpu.make_async_remote_copy(
            wide.at[:, pl.ds(cols, halo)], wide.at[:, pl.ds(0, halo)],
            col_send.at[1], col_recv.at[1], device_id=right, device_id_type=MESH,
        )

    load.wait()
    row_chunk(0)

    @pl.when(has_left)
    def _():
        to_left().start()

    row_chunk(chunks - 1)

    @pl.when(has_right)
    def _():
        to_right().start()

    lax.fori_loop(0, col_lats + 2, prepare_col, 0)

    def interior(chunk, carry):
        row_chunk(chunk)
        return carry

    lax.fori_loop(1, chunks - 1, interior, 0)

    def middle(i, carry):
        col_middle(i)
        return carry

    def finish(k, carry):
        col_final(k)
        return carry

    lax.fori_loop(2, col_lats, middle, 0)
    lax.fori_loop(2, col_lats - 2, finish, 0)
    inner = pl.ds(halo, cols - 2 * halo)
    store_inner = pltpu.make_async_copy(final.at[:, inner], out.at[:, inner], out_sem.at[0])
    store_inner.start()

    @pl.when(has_right)
    def _():
        to_left().wait_recv()

    col_middle(col_lats)
    col_middle(col_lats + 1)
    col_final(col_lats - 2)
    col_final(col_lats - 1)
    high_edge = pl.ds(cols - halo, halo)
    store_high = pltpu.make_async_copy(final.at[:, high_edge], out.at[:, high_edge], out_sem.at[1])
    store_high.start()

    @pl.when(has_left)
    def _():
        to_right().wait_recv()

    col_middle(0)
    col_middle(1)
    col_final(0)
    col_final(1)
    low_edge = pl.ds(0, halo)
    store_low = pltpu.make_async_copy(final.at[:, low_edge], out.at[:, low_edge], out_sem.at[2])
    store_low.start()

    @pl.when(has_down)
    def _():
        for chunk in order:
            to_down(chunk).wait_send()

    @pl.when(has_up)
    def _():
        for chunk in order:
            to_up(chunk).wait_send()

    @pl.when(has_left)
    def _():
        to_left().wait_send()

    @pl.when(has_right)
    def _():
        to_right().wait_send()

    store_inner.wait()
    store_high.wait()
    store_low.wait()


def solution(mesh):
    rows_n, cols_n = mesh.shape["row"], mesh.shape["col"]

    def per_device(covariance, lon_courant, lat_courant, zonal_upwind_sign, lat_sign, cycle_counts):
        rows, cols = covariance.shape
        row_lats, col_lats = rows // NLON, cols // NLON
        chunks = cols // WIDE
        vmem = pl.BlockSpec(memory_space=pltpu.VMEM)
        return pl.pallas_call(
            functools.partial(kernel, rows_n, cols_n),
            out_shape=jax.ShapeDtypeStruct((rows, cols), F32),
            in_specs=[
                pl.BlockSpec(memory_space=pl.ANY), vmem, vmem, vmem, vmem,
                pl.BlockSpec(memory_space=pltpu.SMEM),
            ],
            out_specs=pl.BlockSpec(memory_space=pl.ANY),
            scratch_shapes=[
                pltpu.VMEM((rows + 4 * NLON, cols), F32),
                pltpu.VMEM((rows, cols + 4 * NLON), F32),
                pltpu.VMEM((row_lats + 2, NLON, WIDE), F32),
                pltpu.VMEM((rows, cols + 2 * NLON), F32),
                pltpu.VMEM((rows, cols), F32),
                pltpu.VMEM((row_lats + 2, NLON, NLON), F32),
                pltpu.VMEM((row_lats + 2, NLON, NLON), F32),
                pltpu.VMEM((row_lats + 2, NLON, NLON), BF16),
                pltpu.VMEM((row_lats + 2, NLON, NLON), BF16),
                pltpu.VMEM((col_lats + 2, NLON, NLON), BF16),
                pltpu.VMEM((col_lats + 2, NLON, NLON), BF16),
                pltpu.SemaphoreType.DMA,
                pltpu.SemaphoreType.DMA((2, chunks)),
                pltpu.SemaphoreType.DMA((2, chunks)),
                pltpu.SemaphoreType.DMA((2,)),
                pltpu.SemaphoreType.DMA((2,)),
                pltpu.SemaphoreType.DMA((3,)),
            ],
            name="forecast",
            compiler_params=pltpu.CompilerParams(
                collective_id=0, has_side_effects=True, vmem_limit_bytes=40 * 2**20
            ),
        )(covariance, lon_courant, lat_courant, zonal_upwind_sign, lat_sign, cycle_counts)

    placed = (P("row", "col"), P(), P(), P(), P(), P())
    return jax.shard_map(
        per_device, mesh=mesh, in_specs=placed, out_specs=P("row", "col"), check_vma=False
    )
```

```python
import functools

import jax
import jax.numpy as jnp
from jax import lax
from jax.experimental import pallas as pl
from jax.experimental.pallas import tpu as pltpu
from jax.sharding import PartitionSpec as P

MESH = pl.DeviceIdType.MESH
NLAT = 128
NLON = 128
SUBCYCLES = 4
WIDE = 256
RELAYED = (5, 6, 8, 9)
F32 = jnp.float32
BF16 = jnp.bfloat16


def split(values):
    high = values.astype(BF16)
    return high, (values - high.astype(F32)).astype(BF16)


def dot(a, b):
    return jnp.dot(a, b, preferred_element_type=F32)


def upwind(center, below, above, courant, from_below):
    nearby = jnp.where(from_below, below, above)
    return center - courant * (center - nearby)


def sweep_matrix(lat, lon_ref, zonal_ref, counts_ref):
    rate = lon_ref[pl.ds(lat, 1), :]
    west = jnp.broadcast_to(zonal_ref[pl.ds(lat, 1), :], (NLON, NLON)) == 1
    count = counts_ref[lat]
    row = lax.broadcasted_iota(jnp.int32, (NLON, NLON), 0)
    column = lax.broadcasted_iota(jnp.int32, (NLON, NLON), 1)
    current = jnp.where(row == column, 1.0, 0.0).astype(F32)
    for cycle in range(SUBCYCLES):
        cell_rate = jnp.where(cycle < count, rate, 0.0)
        nearby = jnp.where(
            west, pltpu.roll(current, 1, 1), pltpu.roll(current, NLON - 1, 1)
        )
        current = current - cell_rate * (current - nearby)
    return current


def kernel(
    rows_n, cols_n,
    cov, lon_hbm, lat_hbm, zonal_hbm, sign_hbm, counts_hbm,
    final,
    ext, wide, relayed, row_mid, col_mid,
    lon_ref, lat_ref, zonal_ref, sign_ref, counts_ref,
    row_rate, row_sign, row_hi, row_lo, col_hi, col_lo,
    load_sem, table_sem, row_send, row_recv, relay_recv, relay_send, col_send, col_recv,
):
    r, c = lax.axis_index("row"), lax.axis_index("col")
    rows, cols = cov.shape
    row_lats, col_lats = rows // NLON, cols // NLON
    halo = 2 * NLON
    inner = cols // WIDE - 2
    first_row, first_col = r * row_lats, c * col_lats
    has_down, has_up = r > 0, r < rows_n - 1
    has_left, has_right = c > 0, c < cols_n - 1
    down, up = (r - 1, c), (r + 1, c)
    left, right = (r, c - 1), (r, c + 1)

    half = rows_n // 2
    below_gap, above_gap = r == half - 1, r == half
    bottom, top = r == 0, r == rows_n - 1
    via_top = (rows_n - 1, c)
    via_bottom = (0, c)
    to_below_gap, to_above_gap = (half - 1, c), (half, c)

    barrier = pltpu.get_barrier_semaphore()
    links = (
        (has_down, down), (has_up, up), (has_left, left), (has_right, right),
        (below_gap, via_top), (top, to_below_gap), (top, to_above_gap), (above_gap, via_top),
        (above_gap, via_bottom), (bottom, to_above_gap), (bottom, to_below_gap), (below_gap, via_bottom),
    )
    for exists, device in links:
        @pl.when(exists)
        def _():
            pl.semaphore_signal(barrier, inc=1, device_id=device, device_id_type=MESH)

    tables = [
        pltpu.make_async_copy(source, target, table_sem.at[i])
        for i, (source, target) in enumerate((
            (lat_hbm, lat_ref), (sign_hbm, sign_ref), (lon_hbm, lon_ref),
            (zonal_hbm, zonal_ref), (counts_hbm, counts_ref),
        ))
    ]
    for table in tables:
        table.start()
    load = pltpu.make_async_copy(cov, ext.at[pl.ds(halo, rows), :], load_sem)
    load.start()

    pl.semaphore_wait(barrier, sum(exists.astype(jnp.int32) for exists, _ in links))

    def piece_columns(piece):
        if piece < 4:
            lat = (0, 1, col_lats - 2, col_lats - 1)[piece]
            return pl.ds(lat * NLON, NLON)
        return inner_columns(piece - 4)

    def inner_columns(chunk):
        return pl.ds(pl.multiple_of((chunk + 1) * WIDE, WIDE), WIDE)

    def to_down(piece, at):
        return pltpu.make_async_remote_copy(
            cov.at[pl.ds(0, halo), at], ext.at[pl.ds(halo + rows, halo), at],
            row_send.at[0, piece], row_recv.at[0, piece],
            device_id=down, device_id_type=MESH,
        )

    def to_up(piece, at):
        return pltpu.make_async_remote_copy(
            cov.at[pl.ds(rows - halo, halo), at], ext.at[pl.ds(0, halo), at],
            row_send.at[1, piece], row_recv.at[1, piece],
            device_id=up, device_id_type=MESH,
        )

    def to_relay(piece, at, rising):
        return pltpu.make_async_remote_copy(
            cov.at[pl.ds(rows - halo if rising else 0, halo), at], relayed.at[:, at],
            row_send.at[int(rising), piece], relay_recv.at[piece],
            device_id=via_top if rising else via_bottom, device_id_type=MESH,
        )

    def from_relay(piece, at, rising):
        return pltpu.make_async_remote_copy(
            relayed.at[:, at], ext.at[pl.ds(0 if rising else halo + rows, halo), at],
            relay_send.at[piece], row_recv.at[int(rising), piece],
            device_id=to_above_gap if rising else to_below_gap, device_id_type=MESH,
        )

    order = (0, 3, 1, 2, *range(4, 4 + inner))
    for piece in order:
        at = piece_columns(piece)
        if piece in RELAYED:
            @pl.when(above_gap)
            def _():
                to_relay(piece, at, False).start()

            @pl.when(below_gap)
            def _():
                to_relay(piece, at, True).start()

            @pl.when(jnp.logical_and(has_down, jnp.logical_not(above_gap)))
            def _():
                to_down(piece, at).start()

            @pl.when(jnp.logical_and(has_up, jnp.logical_not(below_gap)))
            def _():
                to_up(piece, at).start()
        else:
            @pl.when(has_down)
            def _():
                to_down(piece, at).start()

            @pl.when(has_up)
            def _():
                to_up(piece, at).start()

    @pl.when(jnp.logical_not(has_down))
    def _():
        ext[pl.ds(0, halo), :] = jnp.zeros((halo, cols), F32)

    @pl.when(jnp.logical_not(has_up))
    def _():
        ext[pl.ds(halo + rows, halo), :] = jnp.zeros((halo, cols), F32)

    @pl.when(jnp.logical_not(has_left))
    def _():
        wide[:, pl.ds(0, halo)] = jnp.zeros((rows, halo), F32)

    @pl.when(jnp.logical_not(has_right))
    def _():
        wide[:, pl.ds(halo + cols, halo)] = jnp.zeros((rows, halo), F32)

    def clamped(lat):
        return jnp.clip(lat, 0, NLAT - 1)

    def courant_of(lat):
        inside = jnp.logical_and(lat >= 0, lat < NLAT)
        return jnp.where(inside, lat_ref[pl.ds(clamped(lat), 1), :], 0.0)

    for table in tables:
        table.wait()

    def prepare_row(i, carry):
        lat = first_row - 1 + i
        at = clamped(lat)
        row_rate[i] = jnp.broadcast_to(courant_of(lat), (NLON, NLON)).T
        row_sign[i] = jnp.broadcast_to(
            sign_ref[pl.ds(at, 1), :].astype(F32), (NLON, NLON)
        ).T
        high, low = split(sweep_matrix(at, lon_ref, zonal_ref, counts_ref).T)
        row_hi[i] = high
        row_lo[i] = low
        return carry

    lax.fori_loop(0, row_lats + 2, prepare_row, 0)

    def prepare_col(i, carry):
        at = clamped(first_col - 1 + i)
        high, low = split(sweep_matrix(at, lon_ref, zonal_ref, counts_ref))
        col_hi[i] = high
        col_lo[i] = low
        return carry

    def row_chunk(piece, start, width):
        at = pl.ds(start, width)

        @pl.when(has_down)
        def _():
            to_up(piece, at).wait_recv()

        @pl.when(has_up)
        def _():
            to_down(piece, at).wait_recv()

        def across(table):
            return jnp.concatenate([table] * (width // NLON), axis=1)

        for i in range(row_lats + 2):
            below = ext[pl.ds(i * NLON, NLON), at]
            center = ext[pl.ds((i + 1) * NLON, NLON), at]
            above = ext[pl.ds((i + 2) * NLON, NLON), at]
            moved = upwind(center, below, above, across(row_rate[i]), across(row_sign[i]) == 1.0)
            high, low = split(moved)
            row_mid[i, :, pl.ds(0, width)] = (
                dot(row_hi[i], high) + (dot(row_hi[i], low) + dot(row_lo[i], high))
            )
        mids = [row_mid[i, :, pl.ds(0, width)] for i in range(row_lats + 2)]
        own = pl.ds(pl.multiple_of(halo + start, NLON), width)
        for i in range(1, row_lats + 1):
            wide[pl.ds((i - 1) * NLON, NLON), own] = upwind(
                mids[i], mids[i - 1], mids[i + 1],
                across(row_rate[i]), across(row_sign[i]) == 1.0,
            )

    def lat_columns(index):
        return pl.ds(pl.multiple_of(index * NLON, NLON), NLON)

    def col_middle(i):
        lat = first_col - 1 + i
        from_below = sign_ref[pl.ds(clamped(lat), 1), :] == 1
        moved = upwind(
            wide[:, lat_columns(i + 1)], wide[:, lat_columns(i)], wide[:, lat_columns(i + 2)],
            courant_of(lat), from_below,
        )
        high, low = split(moved)
        col_mid[:, lat_columns(i)] = (
            dot(high, col_hi[i]) + (dot(low, col_hi[i]) + dot(high, col_lo[i]))
        )

    def col_final(k):
        lat = first_col + k
        from_below = sign_ref[pl.ds(lat, 1), :] == 1
        final[:, lat_columns(k)] = upwind(
            col_mid[:, lat_columns(k + 1)], col_mid[:, lat_columns(k)],
            col_mid[:, lat_columns(k + 2)], courant_of(lat), from_below,
        )

    def to_left(lat):
        return pltpu.make_async_remote_copy(
            wide.at[:, pl.ds(halo + lat * NLON, NLON)],
            wide.at[:, pl.ds(halo + cols + lat * NLON, NLON)],
            col_send.at[0, lat], col_recv.at[0, lat], device_id=left, device_id_type=MESH,
        )

    def to_right(lat):
        return pltpu.make_async_remote_copy(
            wide.at[:, pl.ds(cols + lat * NLON, NLON)],
            wide.at[:, pl.ds(lat * NLON, NLON)],
            col_send.at[1, lat], col_recv.at[1, lat], device_id=right, device_id_type=MESH,
        )

    def pass_on(piece, at):
        @pl.when(top)
        def _():
            to_relay(piece, at, True).wait_recv()
            from_relay(piece, at, True).start()

        @pl.when(bottom)
        def _():
            to_relay(piece, at, False).wait_recv()
            from_relay(piece, at, False).start()

    load.wait()
    for piece in (0, 3, 1, 2):
        lat = (0, 1, col_lats - 2, col_lats - 1)[piece]
        row_chunk(piece, lat * NLON, NLON)
        if piece < 2:
            @pl.when(has_left)
            def _():
                to_left(piece).start()
        else:
            @pl.when(has_right)
            def _():
                to_right(piece - 2).start()

    lax.fori_loop(0, col_lats + 2, prepare_col, 0)

    def interior(chunk, carry):
        goes_on = functools.reduce(jnp.logical_or, [chunk == piece - 4 for piece in RELAYED])

        @pl.when(goes_on)
        def _():
            pass_on(4 + chunk, inner_columns(chunk))

        row_chunk(4 + chunk, pl.multiple_of((chunk + 1) * WIDE, WIDE), WIDE)
        col_middle(2 * chunk + 2)
        col_middle(2 * chunk + 3)

        @pl.when(chunk > 0)
        def _():
            col_final(2 * chunk)
            col_final(2 * chunk + 1)

        return carry

    lax.fori_loop(0, inner, interior, 0)
    col_middle(2 * inner + 2)
    col_middle(2 * inner + 3)
    for k in range(2 * inner, 2 * inner + 2):
        col_final(k)

    @pl.when(has_right)
    def _():
        to_left(0).wait_recv()
        to_left(1).wait_recv()

    col_middle(col_lats)
    col_middle(col_lats + 1)
    col_final(col_lats - 2)
    col_final(col_lats - 1)

    @pl.when(has_left)
    def _():
        to_right(0).wait_recv()
        to_right(1).wait_recv()

    col_middle(0)
    col_middle(1)
    col_final(0)
    col_final(1)

    for piece in order:
        at = piece_columns(piece)

        @pl.when(has_down)
        def _():
            to_down(piece, at).wait_send()

        @pl.when(has_up)
        def _():
            to_up(piece, at).wait_send()

        if piece in RELAYED:
            @pl.when(jnp.logical_or(top, bottom))
            def _():
                from_relay(piece, at, True).wait_send()

    for lat in range(2):
        @pl.when(has_left)
        def _():
            to_left(lat).wait_send()

        @pl.when(has_right)
        def _():
            to_right(lat).wait_send()


def solution(mesh):
    rows_n, cols_n = mesh.shape["row"], mesh.shape["col"]

    def per_device(covariance, lon_courant, lat_courant, zonal_upwind_sign, lat_sign, cycle_counts):
        rows, cols = covariance.shape
        row_lats, col_lats = rows // NLON, cols // NLON
        pieces = cols // WIDE + 2
        hbm = pl.BlockSpec(memory_space=pltpu.HBM)
        return pl.pallas_call(
            functools.partial(kernel, rows_n, cols_n),
            out_shape=jax.ShapeDtypeStruct((rows, cols), F32),
            in_specs=[hbm] * 6,
            out_specs=pl.BlockSpec(memory_space=pltpu.VMEM),
            scratch_shapes=[
                pltpu.VMEM((rows + 4 * NLON, cols), F32),
                pltpu.VMEM((rows, cols + 4 * NLON), F32),
                pltpu.VMEM((2 * NLON, cols), F32),
                pltpu.VMEM((row_lats + 2, NLON, WIDE), F32),
                pltpu.VMEM((rows, cols + 2 * NLON), F32),
                pltpu.VMEM((NLAT, NLON), F32),
                pltpu.VMEM((NLAT, NLON), F32),
                pltpu.VMEM((NLAT, NLON), jnp.int32),
                pltpu.VMEM((NLAT, NLON), jnp.int32),
                pltpu.SMEM((NLAT,), jnp.int32),
                pltpu.VMEM((row_lats + 2, NLON, NLON), F32),
                pltpu.VMEM((row_lats + 2, NLON, NLON), F32),
                pltpu.VMEM((row_lats + 2, NLON, NLON), BF16),
                pltpu.VMEM((row_lats + 2, NLON, NLON), BF16),
                pltpu.VMEM((col_lats + 2, NLON, NLON), BF16),
                pltpu.VMEM((col_lats + 2, NLON, NLON), BF16),
                pltpu.SemaphoreType.DMA,
                pltpu.SemaphoreType.DMA((5,)),
                pltpu.SemaphoreType.DMA((2, pieces)),
                pltpu.SemaphoreType.DMA((2, pieces)),
                pltpu.SemaphoreType.DMA((pieces,)),
                pltpu.SemaphoreType.DMA((pieces,)),
                pltpu.SemaphoreType.DMA((2, 2)),
                pltpu.SemaphoreType.DMA((2, 2)),
            ],
            name="forecast",
            compiler_params=pltpu.CompilerParams(
                collective_id=0, has_side_effects=True, vmem_limit_bytes=48 * 2**20
            ),
        )(*[pltpu.with_memory_space_constraint(a, pltpu.HBM) for a in (covariance, lon_courant, lat_courant, zonal_upwind_sign, lat_sign, cycle_counts)])

    placed = (P("row", "col"), P(), P(), P(), P(), P())
    return jax.shard_map(
        per_device, mesh=mesh, in_specs=placed, out_specs=P("row", "col"), check_vma=False
    )
```

```python
import functools

import jax
import jax.numpy as jnp
from jax import lax
from jax.experimental import pallas as pl
from jax.experimental.pallas import tpu as pltpu
from jax.sharding import PartitionSpec as P

MESH = pl.DeviceIdType.MESH
NLAT = 128
NLON = 128
SUBCYCLES = 4
WIDE = 256
RELAYS = {4: (31, 0), 5: (31, 0), 6: (19, 12), 7: (21, 10), 8: (28, 3), 9: (26, 5)}
RELAY_TURN = {4: 1, 5: 2, 6: 1, 7: 2, 8: 1, 9: 2}
F32 = jnp.float32
BF16 = jnp.bfloat16


def split(values):
    high = values.astype(BF16)
    return high, (values - high.astype(F32)).astype(BF16)


def dot(a, b):
    return jnp.dot(a, b, preferred_element_type=F32)


def upwind(center, below, above, courant, from_below):
    nearby = jnp.where(from_below, below, above)
    return center - courant * (center - nearby)


def sweep_matrix(lat, lon_ref, zonal_ref, counts_ref):
    rate = lon_ref[pl.ds(lat, 1), :]
    west = jnp.broadcast_to(zonal_ref[pl.ds(lat, 1), :], (NLON, NLON)) == 1
    count = counts_ref[lat]
    row = lax.broadcasted_iota(jnp.int32, (NLON, NLON), 0)
    column = lax.broadcasted_iota(jnp.int32, (NLON, NLON), 1)
    current = jnp.where(row == column, 1.0, 0.0).astype(F32)
    for cycle in range(SUBCYCLES):
        cell_rate = jnp.where(cycle < count, rate, 0.0)
        nearby = jnp.where(
            west, pltpu.roll(current, 1, 1), pltpu.roll(current, NLON - 1, 1)
        )
        current = current - cell_rate * (current - nearby)
    return current


def kernel(
    rows_n, cols_n,
    cov, lon_hbm, lat_hbm, zonal_hbm, sign_hbm, counts_hbm,
    final,
    ext, wide, relayed, row_mid, col_mid,
    lon_ref, lat_ref, zonal_ref, sign_ref, counts_ref,
    row_rate, row_sign, row_hi, row_lo, col_hi, col_lo,
    load_sem, table_sem, row_send, row_recv, relay_recv, relay_send, col_send, col_recv,
):
    r, c = lax.axis_index("row"), lax.axis_index("col")
    rows, cols = cov.shape
    row_lats, col_lats = rows // NLON, cols // NLON
    halo = 2 * NLON
    inner = cols // WIDE - 2
    first_row, first_col = r * row_lats, c * col_lats
    has_down, has_up = r > 0, r < rows_n - 1
    has_left, has_right = c > 0, c < cols_n - 1
    down, up = (r - 1, c), (r + 1, c)
    left, right = (r, c - 1), (r, c + 1)

    half = rows_n // 2
    below_gap, above_gap = r == half - 1, r == half
    to_below_gap, to_above_gap = (half - 1, c), (half, c)

    barrier = pltpu.get_barrier_semaphore()
    links = [(has_down, down), (has_up, up), (has_left, left), (has_right, right)]
    for relay in sorted({relay for pair in RELAYS.values() for relay in pair}):
        links += [
            (below_gap, (relay, c)), (above_gap, (relay, c)),
            (r == relay, to_below_gap), (r == relay, to_above_gap),
        ]
    for exists, device in links:
        @pl.when(exists)
        def _():
            pl.semaphore_signal(barrier, inc=1, device_id=device, device_id_type=MESH)

    tables = [
        pltpu.make_async_copy(source, target, table_sem.at[i])
        for i, (source, target) in enumerate((
            (lat_hbm, lat_ref), (sign_hbm, sign_ref), (lon_hbm, lon_ref),
            (zonal_hbm, zonal_ref), (counts_hbm, counts_ref),
        ))
    ]
    for table in tables:
        table.start()
    load = pltpu.make_async_copy(cov, ext.at[pl.ds(halo, rows), :], load_sem)
    load.start()

    pl.semaphore_wait(barrier, sum(exists.astype(jnp.int32) for exists, _ in links))

    def piece_columns(piece):
        if piece < 4:
            lat = (0, 1, col_lats - 2, col_lats - 1)[piece]
            return pl.ds(lat * NLON, NLON)
        return inner_columns(piece - 4)

    def inner_columns(chunk):
        return pl.ds(pl.multiple_of((chunk + 1) * WIDE, WIDE), WIDE)

    def to_down(piece, at):
        return pltpu.make_async_remote_copy(
            cov.at[pl.ds(0, halo), at], ext.at[pl.ds(halo + rows, halo), at],
            row_send.at[0, piece], row_recv.at[0, piece],
            device_id=down, device_id_type=MESH,
        )

    def to_up(piece, at):
        return pltpu.make_async_remote_copy(
            cov.at[pl.ds(rows - halo, halo), at], ext.at[pl.ds(0, halo), at],
            row_send.at[1, piece], row_recv.at[1, piece],
            device_id=up, device_id_type=MESH,
        )

    def to_relay(piece, at, rising):
        return pltpu.make_async_remote_copy(
            cov.at[pl.ds(rows - halo if rising else 0, halo), at], relayed.at[:, at],
            row_send.at[int(rising), piece], relay_recv.at[piece],
            device_id=(RELAYS[piece][0 if rising else 1], c), device_id_type=MESH,
        )

    def from_relay(piece, at, rising):
        return pltpu.make_async_remote_copy(
            relayed.at[:, at], ext.at[pl.ds(0 if rising else halo + rows, halo), at],
            relay_send.at[piece], row_recv.at[int(rising), piece],
            device_id=to_above_gap if rising else to_below_gap, device_id_type=MESH,
        )

    order = (0, 3, 1, 2, *range(4, 4 + inner))
    for piece in order:
        at = piece_columns(piece)
        if piece in RELAYS:
            @pl.when(above_gap)
            def _():
                to_relay(piece, at, False).start()

            @pl.when(below_gap)
            def _():
                to_relay(piece, at, True).start()

            @pl.when(jnp.logical_and(has_down, jnp.logical_not(above_gap)))
            def _():
                to_down(piece, at).start()

            @pl.when(jnp.logical_and(has_up, jnp.logical_not(below_gap)))
            def _():
                to_up(piece, at).start()
        else:
            @pl.when(has_down)
            def _():
                to_down(piece, at).start()

            @pl.when(has_up)
            def _():
                to_up(piece, at).start()

    @pl.when(jnp.logical_not(has_down))
    def _():
        ext[pl.ds(0, halo), :] = jnp.zeros((halo, cols), F32)

    @pl.when(jnp.logical_not(has_up))
    def _():
        ext[pl.ds(halo + rows, halo), :] = jnp.zeros((halo, cols), F32)

    @pl.when(jnp.logical_not(has_left))
    def _():
        wide[:, pl.ds(0, halo)] = jnp.zeros((rows, halo), F32)

    @pl.when(jnp.logical_not(has_right))
    def _():
        wide[:, pl.ds(halo + cols, halo)] = jnp.zeros((rows, halo), F32)

    def clamped(lat):
        return jnp.clip(lat, 0, NLAT - 1)

    def courant_of(lat):
        inside = jnp.logical_and(lat >= 0, lat < NLAT)
        return jnp.where(inside, lat_ref[pl.ds(clamped(lat), 1), :], 0.0)

    for table in tables:
        table.wait()

    def prepare_row(i, carry):
        lat = first_row - 1 + i
        at = clamped(lat)
        row_rate[i] = jnp.broadcast_to(courant_of(lat), (NLON, NLON)).T
        row_sign[i] = jnp.broadcast_to(
            sign_ref[pl.ds(at, 1), :].astype(F32), (NLON, NLON)
        ).T
        high, low = split(sweep_matrix(at, lon_ref, zonal_ref, counts_ref).T)
        row_hi[i] = high
        row_lo[i] = low
        return carry

    lax.fori_loop(0, row_lats + 2, prepare_row, 0)

    def prepare_col(i, carry):
        at = clamped(first_col - 1 + i)
        high, low = split(sweep_matrix(at, lon_ref, zonal_ref, counts_ref))
        col_hi[i] = high
        col_lo[i] = low
        return carry

    def row_chunk(piece, start, width):
        at = pl.ds(start, width)

        @pl.when(has_down)
        def _():
            to_up(piece, at).wait_recv()

        @pl.when(has_up)
        def _():
            to_down(piece, at).wait_recv()

        def across(table):
            return jnp.concatenate([table] * (width // NLON), axis=1)

        for i in range(row_lats + 2):
            below = ext[pl.ds(i * NLON, NLON), at]
            center = ext[pl.ds((i + 1) * NLON, NLON), at]
            above = ext[pl.ds((i + 2) * NLON, NLON), at]
            moved = upwind(center, below, above, across(row_rate[i]), across(row_sign[i]) == 1.0)
            high, low = split(moved)
            row_mid[i, :, pl.ds(0, width)] = (
                dot(row_hi[i], high) + (dot(row_hi[i], low) + dot(row_lo[i], high))
            )
        mids = [row_mid[i, :, pl.ds(0, width)] for i in range(row_lats + 2)]
        own = pl.ds(pl.multiple_of(halo + start, NLON), width)
        for i in range(1, row_lats + 1):
            wide[pl.ds((i - 1) * NLON, NLON), own] = upwind(
                mids[i], mids[i - 1], mids[i + 1],
                across(row_rate[i]), across(row_sign[i]) == 1.0,
            )

    def lat_columns(index):
        return pl.ds(pl.multiple_of(index * NLON, NLON), NLON)

    def col_middle(i):
        lat = first_col - 1 + i
        from_below = sign_ref[pl.ds(clamped(lat), 1), :] == 1
        moved = upwind(
            wide[:, lat_columns(i + 1)], wide[:, lat_columns(i)], wide[:, lat_columns(i + 2)],
            courant_of(lat), from_below,
        )
        high, low = split(moved)
        col_mid[:, lat_columns(i)] = (
            dot(high, col_hi[i]) + (dot(low, col_hi[i]) + dot(high, col_lo[i]))
        )

    def col_final(k):
        lat = first_col + k
        from_below = sign_ref[pl.ds(lat, 1), :] == 1
        final[:, lat_columns(k)] = upwind(
            col_mid[:, lat_columns(k + 1)], col_mid[:, lat_columns(k)],
            col_mid[:, lat_columns(k + 2)], courant_of(lat), from_below,
        )

    def to_left(lat):
        return pltpu.make_async_remote_copy(
            wide.at[:, pl.ds(halo + lat * NLON, NLON)],
            wide.at[:, pl.ds(halo + cols + lat * NLON, NLON)],
            col_send.at[0, lat], col_recv.at[0, lat], device_id=left, device_id_type=MESH,
        )

    def to_right(lat):
        return pltpu.make_async_remote_copy(
            wide.at[:, pl.ds(cols + lat * NLON, NLON)],
            wide.at[:, pl.ds(lat * NLON, NLON)],
            col_send.at[1, lat], col_recv.at[1, lat], device_id=right, device_id_type=MESH,
        )

    def pass_on(piece):
        at = piece_columns(piece)
        for relay, rising in zip(RELAYS[piece], (True, False)):
            @pl.when(r == relay)
            def _():
                to_relay(piece, at, rising).wait_recv()
                from_relay(piece, at, rising).start()

    load.wait()
    for piece in (0, 3, 1, 2):
        lat = (0, 1, col_lats - 2, col_lats - 1)[piece]
        row_chunk(piece, lat * NLON, NLON)
        if piece < 2:
            @pl.when(has_left)
            def _():
                to_left(piece).start()
        else:
            @pl.when(has_right)
            def _():
                to_right(piece - 2).start()

    lax.fori_loop(0, col_lats + 2, prepare_col, 0)

    def interior(chunk, carry):
        for turn in sorted(set(RELAY_TURN.values())):
            @pl.when(chunk == turn)
            def _():
                for piece in RELAYS:
                    if RELAY_TURN[piece] == turn:
                        pass_on(piece)

        row_chunk(4 + chunk, pl.multiple_of((chunk + 1) * WIDE, WIDE), WIDE)
        col_middle(2 * chunk + 2)
        col_middle(2 * chunk + 3)

        @pl.when(chunk > 0)
        def _():
            col_final(2 * chunk)
            col_final(2 * chunk + 1)

        return carry

    lax.fori_loop(0, inner, interior, 0)
    col_middle(2 * inner + 2)
    col_middle(2 * inner + 3)
    for k in range(2 * inner, 2 * inner + 2):
        col_final(k)

    @pl.when(has_right)
    def _():
        to_left(0).wait_recv()
        to_left(1).wait_recv()

    col_middle(col_lats)
    col_middle(col_lats + 1)
    col_final(col_lats - 2)
    col_final(col_lats - 1)

    @pl.when(has_left)
    def _():
        to_right(0).wait_recv()
        to_right(1).wait_recv()

    col_middle(0)
    col_middle(1)
    col_final(0)
    col_final(1)

    for piece in order:
        at = piece_columns(piece)

        @pl.when(has_down)
        def _():
            to_down(piece, at).wait_send()

        @pl.when(has_up)
        def _():
            to_up(piece, at).wait_send()

        if piece in RELAYS:
            for relay, rising in zip(RELAYS[piece], (True, False)):
                @pl.when(r == relay)
                def _():
                    from_relay(piece, at, rising).wait_send()

    for lat in range(2):
        @pl.when(has_left)
        def _():
            to_left(lat).wait_send()

        @pl.when(has_right)
        def _():
            to_right(lat).wait_send()


def solution(mesh):
    rows_n, cols_n = mesh.shape["row"], mesh.shape["col"]

    def per_device(covariance, lon_courant, lat_courant, zonal_upwind_sign, lat_sign, cycle_counts):
        rows, cols = covariance.shape
        row_lats, col_lats = rows // NLON, cols // NLON
        pieces = cols // WIDE + 2
        hbm = pl.BlockSpec(memory_space=pltpu.HBM)
        return pl.pallas_call(
            functools.partial(kernel, rows_n, cols_n),
            out_shape=jax.ShapeDtypeStruct((rows, cols), F32),
            in_specs=[hbm] * 6,
            out_specs=pl.BlockSpec(memory_space=pltpu.VMEM),
            scratch_shapes=[
                pltpu.VMEM((rows + 4 * NLON, cols), F32),
                pltpu.VMEM((rows, cols + 4 * NLON), F32),
                pltpu.VMEM((2 * NLON, cols), F32),
                pltpu.VMEM((row_lats + 2, NLON, WIDE), F32),
                pltpu.VMEM((rows, cols + 2 * NLON), F32),
                pltpu.VMEM((NLAT, NLON), F32),
                pltpu.VMEM((NLAT, NLON), F32),
                pltpu.VMEM((NLAT, NLON), jnp.int32),
                pltpu.VMEM((NLAT, NLON), jnp.int32),
                pltpu.SMEM((NLAT,), jnp.int32),
                pltpu.VMEM((row_lats + 2, NLON, NLON), F32),
                pltpu.VMEM((row_lats + 2, NLON, NLON), F32),
                pltpu.VMEM((row_lats + 2, NLON, NLON), BF16),
                pltpu.VMEM((row_lats + 2, NLON, NLON), BF16),
                pltpu.VMEM((col_lats + 2, NLON, NLON), BF16),
                pltpu.VMEM((col_lats + 2, NLON, NLON), BF16),
                pltpu.SemaphoreType.DMA,
                pltpu.SemaphoreType.DMA((5,)),
                pltpu.SemaphoreType.DMA((2, pieces)),
                pltpu.SemaphoreType.DMA((2, pieces)),
                pltpu.SemaphoreType.DMA((pieces,)),
                pltpu.SemaphoreType.DMA((pieces,)),
                pltpu.SemaphoreType.DMA((2, 2)),
                pltpu.SemaphoreType.DMA((2, 2)),
            ],
            name="forecast",
            compiler_params=pltpu.CompilerParams(
                collective_id=0, has_side_effects=True, vmem_limit_bytes=48 * 2**20
            ),
        )(*[pltpu.with_memory_space_constraint(a, pltpu.HBM) for a in (covariance, lon_courant, lat_courant, zonal_upwind_sign, lat_sign, cycle_counts)])

    placed = (P("row", "col"), P(), P(), P(), P(), P())
    return jax.shard_map(
        per_device, mesh=mesh, in_specs=placed, out_specs=P("row", "col"), check_vma=False
    )
```

```python
import functools

import jax
import jax.numpy as jnp
from jax import lax
from jax.experimental import pallas as pl
from jax.experimental.pallas import tpu as pltpu
from jax.sharding import PartitionSpec as P

MESH = pl.DeviceIdType.MESH
NLAT = 128
NLON = 128
SUBCYCLES = 4
EDGE_LATS = (-1, 0, 1, 14, 15, 16)
WIDE = 256
RELAYS = {4: (31, 12), 5: (31, 12), 6: (19, 10), 7: (21, 3), 8: (28, 5), 9: (26, 7), 10: (26, None)}
RELAY_TURN = {4: 1, 5: 1, 6: 1, 7: 2, 8: 1, 9: 2, 10: 2}
F32 = jnp.float32
BF16 = jnp.bfloat16


def split(values):
    high = values.astype(BF16)
    return high, (values - high.astype(F32)).astype(BF16)


def dot(a, b):
    return jnp.dot(a, b, preferred_element_type=F32)


def upwind(center, below, above, courant, from_below):
    nearby = jnp.where(from_below, below, above)
    return center - courant * (center - nearby)


def sweep_matrix(lat, lon_ref, zonal_ref, counts_ref):
    rate = lon_ref[pl.ds(lat, 1), :]
    west = jnp.broadcast_to(zonal_ref[pl.ds(lat, 1), :], (NLON, NLON)) == 1
    count = counts_ref[lat]
    row = lax.broadcasted_iota(jnp.int32, (NLON, NLON), 0)
    column = lax.broadcasted_iota(jnp.int32, (NLON, NLON), 1)
    current = jnp.where(row == column, 1.0, 0.0).astype(F32)
    for cycle in range(SUBCYCLES):
        cell_rate = jnp.where(cycle < count, rate, 0.0)
        nearby = jnp.where(
            west, pltpu.roll(current, 1, 1), pltpu.roll(current, NLON - 1, 1)
        )
        current = current - cell_rate * (current - nearby)
    return current


def kernel(
    rows_n, cols_n,
    cov, lon_hbm, lat_hbm, zonal_hbm, sign_hbm, counts_hbm,
    final, wide, col_mid, col_hi, col_lo, edge_rows,
    ext, relayed, row_mid,
    lon_ref, lat_ref, zonal_ref, sign_ref, counts_ref,
    row_rate, row_sign, row_hi, row_lo,
    load_sem, table_sem, row_send, row_recv, relay_recv, relay_send, col_send, col_recv,
):
    r, c = lax.axis_index("row"), lax.axis_index("col")
    rows, cols = cov.shape
    row_lats, col_lats = rows // NLON, cols // NLON
    halo = 2 * NLON
    inner = cols // WIDE - 3
    pieces = inner + 6
    first_row, first_col = r * row_lats, c * col_lats
    has_down, has_up = r > 0, r < rows_n - 1
    has_left, has_right = c > 0, c < cols_n - 1
    down, up = (r - 1, c), (r + 1, c)
    left, right = (r, c - 1), (r, c + 1)

    half = rows_n // 2
    below_gap, above_gap = r == half - 1, r == half
    to_below_gap, to_above_gap = (half - 1, c), (half, c)

    barrier = pltpu.get_barrier_semaphore()
    links = [(has_down, down), (has_up, up), (has_left, left), (has_right, right)]
    for relay in sorted({relay for pair in RELAYS.values() for relay in pair if relay is not None}):
        links += [
            (below_gap, (relay, c)), (above_gap, (relay, c)),
            (r == relay, to_below_gap), (r == relay, to_above_gap),
        ]
    for exists, device in links:
        @pl.when(exists)
        def _():
            pl.semaphore_signal(barrier, inc=1, device_id=device, device_id_type=MESH)

    tables = [
        pltpu.make_async_copy(source, target, table_sem.at[i])
        for i, (source, target) in enumerate((
            (lat_hbm, lat_ref), (sign_hbm, sign_ref), (lon_hbm, lon_ref),
            (zonal_hbm, zonal_ref), (counts_hbm, counts_ref),
        ))
    ]
    for table in tables:
        table.start()
    load = pltpu.make_async_copy(cov, ext.at[pl.ds(halo, rows), :], load_sem)
    load.start()

    pl.semaphore_wait(barrier, sum(exists.astype(jnp.int32) for exists, _ in links))

    def piece_columns(piece):
        if piece < 4:
            lat = (0, 1, col_lats - 2, col_lats - 1)[piece]
            return pl.ds(lat * NLON, NLON)
        if piece < 4 + inner:
            return inner_columns(piece - 4)
        return pl.ds(inner_end + (piece - 4 - inner) * NLON, NLON)

    inner_end = (inner + 1) * WIDE

    def inner_columns(chunk):
        return pl.ds(pl.multiple_of((chunk + 1) * WIDE, WIDE), WIDE)

    def to_down(piece, at):
        return pltpu.make_async_remote_copy(
            cov.at[pl.ds(0, halo), at], ext.at[pl.ds(halo + rows, halo), at],
            row_send.at[0, piece], row_recv.at[0, piece],
            device_id=down, device_id_type=MESH,
        )

    def to_up(piece, at):
        return pltpu.make_async_remote_copy(
            cov.at[pl.ds(rows - halo, halo), at], ext.at[pl.ds(0, halo), at],
            row_send.at[1, piece], row_recv.at[1, piece],
            device_id=up, device_id_type=MESH,
        )

    def to_relay(piece, at, rising):
        return pltpu.make_async_remote_copy(
            cov.at[pl.ds(rows - halo if rising else 0, halo), at], relayed.at[:, at],
            row_send.at[int(rising), piece], relay_recv.at[piece],
            device_id=(RELAYS[piece][0 if rising else 1], c), device_id_type=MESH,
        )

    def from_relay(piece, at, rising):
        return pltpu.make_async_remote_copy(
            relayed.at[:, at], ext.at[pl.ds(0 if rising else halo + rows, halo), at],
            relay_send.at[piece], row_recv.at[int(rising), piece],
            device_id=to_above_gap if rising else to_below_gap, device_id_type=MESH,
        )

    order = (0, 3, 1, 2, *range(4, pieces))
    for piece in order:
        at = piece_columns(piece)
        by_top, by_bottom = RELAYS.get(piece, (None, None))
        for relay, rising, gap, exists, direct in (
            (by_bottom, False, above_gap, has_down, to_down),
            (by_top, True, below_gap, has_up, to_up),
        ):
            if relay is None:
                @pl.when(exists)
                def _():
                    direct(piece, at).start()
            else:
                @pl.when(gap)
                def _():
                    to_relay(piece, at, rising).start()

                @pl.when(jnp.logical_and(exists, jnp.logical_not(gap)))
                def _():
                    direct(piece, at).start()

    @pl.when(jnp.logical_not(has_down))
    def _():
        ext[pl.ds(0, halo), :] = jnp.zeros((halo, cols), F32)

    @pl.when(jnp.logical_not(has_up))
    def _():
        ext[pl.ds(halo + rows, halo), :] = jnp.zeros((halo, cols), F32)

    @pl.when(jnp.logical_not(has_left))
    def _():
        wide[:, pl.ds(0, halo)] = jnp.zeros((rows, halo), F32)

    @pl.when(jnp.logical_not(has_right))
    def _():
        wide[:, pl.ds(halo + cols, halo)] = jnp.zeros((rows, halo), F32)

    def clamped(lat):
        return jnp.clip(lat, 0, NLAT - 1)

    def courant_of(lat):
        inside = jnp.logical_and(lat >= 0, lat < NLAT)
        return jnp.where(inside, lat_ref[pl.ds(clamped(lat), 1), :], 0.0)

    for table in tables:
        table.wait()

    def prepare_row(i, carry):
        lat = first_row - 1 + i
        at = clamped(lat)
        row_rate[i] = jnp.broadcast_to(courant_of(lat), (NLON, NLON)).T
        row_sign[i] = jnp.broadcast_to(
            sign_ref[pl.ds(at, 1), :].astype(F32), (NLON, NLON)
        ).T
        high, low = split(sweep_matrix(at, lon_ref, zonal_ref, counts_ref).T)
        row_hi[i] = high
        row_lo[i] = low
        return carry

    lax.fori_loop(0, row_lats + 2, prepare_row, 0, unroll=3)

    def prepare_col(i, carry):
        at = clamped(first_col - 1 + i)
        high, low = split(sweep_matrix(at, lon_ref, zonal_ref, counts_ref))
        col_hi[i] = high
        col_lo[i] = low
        return carry

    def row_chunk(piece, start, width):
        at = pl.ds(start, width)

        @pl.when(has_down)
        def _():
            to_up(piece, at).wait_recv()

        @pl.when(has_up)
        def _():
            to_down(piece, at).wait_recv()

        def across(table):
            return jnp.concatenate([table] * (width // NLON), axis=1)

        for i in range(row_lats + 2):
            below = ext[pl.ds(i * NLON, NLON), at]
            center = ext[pl.ds((i + 1) * NLON, NLON), at]
            above = ext[pl.ds((i + 2) * NLON, NLON), at]
            moved = upwind(center, below, above, across(row_rate[i]), across(row_sign[i]) == 1.0)
            high, low = split(moved)
            row_mid[i, :, pl.ds(0, width)] = (
                dot(row_hi[i], high) + (dot(row_hi[i], low) + dot(row_lo[i], high))
            )
        mids = [row_mid[i, :, pl.ds(0, width)] for i in range(row_lats + 2)]
        own = pl.ds(pl.multiple_of(halo + start, NLON), width)
        for i in range(1, row_lats + 1):
            wide[pl.ds((i - 1) * NLON, NLON), own] = upwind(
                mids[i], mids[i - 1], mids[i + 1],
                across(row_rate[i]), across(row_sign[i]) == 1.0,
            )

    def lat_columns(index):
        return pl.ds(pl.multiple_of(index * NLON, NLON), NLON)

    def col_middle(i):
        lat = first_col - 1 + i
        from_below = sign_ref[pl.ds(clamped(lat), 1), :] == 1
        moved = upwind(
            wide[:, lat_columns(i + 1)], wide[:, lat_columns(i)], wide[:, lat_columns(i + 2)],
            courant_of(lat), from_below,
        )
        high, low = split(moved)
        col_mid[:, lat_columns(i)] = (
            dot(high, col_hi[i]) + (dot(low, col_hi[i]) + dot(high, col_lo[i]))
        )

    def col_final(k):
        lat = first_col + k
        from_below = sign_ref[pl.ds(lat, 1), :] == 1
        final[:, lat_columns(k)] = upwind(
            col_mid[:, lat_columns(k + 1)], col_mid[:, lat_columns(k)],
            col_mid[:, lat_columns(k + 2)], courant_of(lat), from_below,
        )

    def to_left(lat):
        return pltpu.make_async_remote_copy(
            wide.at[:, pl.ds(halo + lat * NLON, NLON)],
            wide.at[:, pl.ds(halo + cols + lat * NLON, NLON)],
            col_send.at[0, lat], col_recv.at[0, lat], device_id=left, device_id_type=MESH,
        )

    def to_right(lat):
        return pltpu.make_async_remote_copy(
            wide.at[:, pl.ds(cols + lat * NLON, NLON)],
            wide.at[:, pl.ds(lat * NLON, NLON)],
            col_send.at[1, lat], col_recv.at[1, lat], device_id=right, device_id_type=MESH,
        )

    def pass_on(piece):
        at = piece_columns(piece)
        for relay, rising in zip(RELAYS[piece], (True, False)):
            if relay is None:
                continue

            @pl.when(r == relay)
            def _():
                to_relay(piece, at, rising).wait_recv()
                from_relay(piece, at, rising).start()

    load.wait()
    for piece in (0, 3, 1, 2):
        lat = (0, 1, col_lats - 2, col_lats - 1)[piece]
        if piece in RELAYS:
            pass_on(piece)
        row_chunk(piece, lat * NLON, NLON)
        if piece < 2:
            @pl.when(has_left)
            def _():
                to_left(piece).start()
        else:
            @pl.when(has_right)
            def _():
                to_right(piece - 2).start()

    lax.fori_loop(0, col_lats + 2, prepare_col, 0, unroll=3)

    def interior(chunk, carry):
        for turn in sorted(set(RELAY_TURN.values())):
            @pl.when(chunk == turn)
            def _():
                for piece in RELAY_TURN:
                    if RELAY_TURN[piece] == turn:
                        pass_on(piece)

        row_chunk(4 + chunk, pl.multiple_of((chunk + 1) * WIDE, WIDE), WIDE)
        col_middle(2 * chunk + 2)
        col_middle(2 * chunk + 3)

        @pl.when(chunk > 0)
        def _():
            col_final(2 * chunk)
            col_final(2 * chunk + 1)

        return carry

    lax.fori_loop(0, inner, interior, 0)

    for i, lat in enumerate(EDGE_LATS):
        edge_rows[pl.ds(i, 1), :] = courant_of(first_col + lat)
        edge_rows[pl.ds(8 + i, 1), :] = sign_ref[
            pl.ds(clamped(first_col + lat), 1), :
        ].astype(F32)

    row_chunk(pieces - 2, inner_end, NLON)
    col_middle(col_lats - 4)
    col_final(col_lats - 6)
    row_chunk(pieces - 1, inner_end + NLON, NLON)
    for i in range(col_lats - 3, col_lats):
        col_middle(i)
    for k in range(col_lats - 5, col_lats - 2):
        col_final(k)

    @pl.when(has_right)
    def _():
        to_left(0).wait_recv()
        to_left(1).wait_recv()

    @pl.when(has_left)
    def _():
        to_right(0).wait_recv()
        to_right(1).wait_recv()

    for piece in order:
        at = piece_columns(piece)

        @pl.when(has_down)
        def _():
            to_down(piece, at).wait_send()

        @pl.when(has_up)
        def _():
            to_up(piece, at).wait_send()

        if piece in RELAYS:
            for relay, rising in zip(RELAYS[piece], (True, False)):
                if relay is None:
                    continue

                @pl.when(r == relay)
                def _():
                    from_relay(piece, at, rising).wait_send()

    for lat in range(2):
        @pl.when(has_left)
        def _():
            to_left(lat).wait_send()

        @pl.when(has_right)
        def _():
            to_right(lat).wait_send()


def finish(
    final, wide, col_mid, col_hi, col_lo, edge_rows, out, edge_mid, edge_final, sems
):
    rows, cols = final.shape
    col_lats = cols // NLON
    edge = 2 * NLON
    inner = pl.ds(edge, cols - 2 * edge)
    stores = [pltpu.make_async_copy(final.at[:, inner], out.at[:, inner], sems.at[0])]
    stores[0].start()

    def lat_columns(index):
        return pl.ds(index * NLON, NLON)

    def row_of(lat):
        at = EDGE_LATS.index(lat)
        return edge_rows[pl.ds(at, 1), :], edge_rows[pl.ds(8 + at, 1), :] == 1.0

    def middle(lat):
        moved = upwind(
            wide[:, lat_columns(lat + 2)], wide[:, lat_columns(lat + 1)],
            wide[:, lat_columns(lat + 3)], *row_of(lat),
        )
        high, low = split(moved)
        i = lat + 1
        return dot(high, col_hi[i]) + (dot(low, col_hi[i]) + dot(high, col_lo[i]))

    for side, (outer, near) in enumerate((((-1, 0), (1, 2)), ((col_lats, col_lats - 1), (col_lats - 2, col_lats - 3)))):
        for at, lat in enumerate(outer):
            edge_mid[side, at] = middle(lat)
        mids = {lat: edge_mid[side, at] for at, lat in enumerate(outer)}
        mids |= {lat: col_mid[:, lat_columns(lat + 1)] for lat in near}
        first = 0 if side == 0 else cols - edge
        for lat in (outer[1], near[0]):
            place = lat * NLON - first
            edge_final[side, :, pl.ds(place, NLON)] = upwind(
                mids[lat], mids[lat - 1], mids[lat + 1], *row_of(lat)
            )
        store = pltpu.make_async_copy(
            edge_final.at[side], out.at[:, pl.ds(first, edge)], sems.at[1 + side]
        )
        store.start()
        stores.append(store)
    for store in stores:
        store.wait()


def solution(mesh):
    rows_n, cols_n = mesh.shape["row"], mesh.shape["col"]

    def per_device(covariance, lon_courant, lat_courant, zonal_upwind_sign, lat_sign, cycle_counts):
        rows, cols = covariance.shape
        row_lats, col_lats = rows // NLON, cols // NLON
        pieces = cols // WIDE + 3
        hbm = pl.BlockSpec(memory_space=pltpu.HBM)
        vmem = pl.BlockSpec(memory_space=pltpu.VMEM)
        parts = pl.pallas_call(
            functools.partial(kernel, rows_n, cols_n),
            out_shape=[
                jax.ShapeDtypeStruct((rows, cols), F32),
                jax.ShapeDtypeStruct((rows, cols + 4 * NLON), F32),
                jax.ShapeDtypeStruct((rows, cols + 2 * NLON), F32),
                jax.ShapeDtypeStruct((col_lats + 2, NLON, NLON), BF16),
                jax.ShapeDtypeStruct((col_lats + 2, NLON, NLON), BF16),
                jax.ShapeDtypeStruct((16, NLON), F32),
            ],
            in_specs=[hbm] * 6,
            out_specs=[vmem] * 6,
            scratch_shapes=[
                pltpu.VMEM((rows + 4 * NLON, cols), F32),
                pltpu.VMEM((2 * NLON, cols), F32),
                pltpu.VMEM((row_lats + 2, NLON, WIDE), F32),
                pltpu.VMEM((NLAT, NLON), F32),
                pltpu.VMEM((NLAT, NLON), F32),
                pltpu.VMEM((NLAT, NLON), jnp.int32),
                pltpu.VMEM((NLAT, NLON), jnp.int32),
                pltpu.SMEM((NLAT,), jnp.int32),
                pltpu.VMEM((row_lats + 2, NLON, NLON), F32),
                pltpu.VMEM((row_lats + 2, NLON, NLON), F32),
                pltpu.VMEM((row_lats + 2, NLON, NLON), BF16),
                pltpu.VMEM((row_lats + 2, NLON, NLON), BF16),
                pltpu.SemaphoreType.DMA,
                pltpu.SemaphoreType.DMA((5,)),
                pltpu.SemaphoreType.DMA((2, pieces)),
                pltpu.SemaphoreType.DMA((2, pieces)),
                pltpu.SemaphoreType.DMA((pieces,)),
                pltpu.SemaphoreType.DMA((pieces,)),
                pltpu.SemaphoreType.DMA((2, 2)),
                pltpu.SemaphoreType.DMA((2, 2)),
            ],
            name="forecast",
            compiler_params=pltpu.CompilerParams(
                collective_id=0, has_side_effects=True, vmem_limit_bytes=36 * 2**20
            ),
        )(*[pltpu.with_memory_space_constraint(a, pltpu.HBM) for a in (covariance, lon_courant, lat_courant, zonal_upwind_sign, lat_sign, cycle_counts)])
        return pl.pallas_call(
            finish,
            out_shape=jax.ShapeDtypeStruct((rows, cols), F32),
            in_specs=[vmem] * 6,
            out_specs=hbm,
            scratch_shapes=[
                pltpu.VMEM((2, 2, rows, NLON), F32),
                pltpu.VMEM((2, rows, 2 * NLON), F32),
                pltpu.SemaphoreType.DMA((3,)),
            ],
            name="finish",
            compiler_params=pltpu.CompilerParams(vmem_limit_bytes=36 * 2**20),
        )(*parts)

    placed = (P("row", "col"), P(), P(), P(), P(), P())
    return jax.shard_map(
        per_device, mesh=mesh, in_specs=placed, out_specs=P("row", "col"), check_vma=False
    )
```

```python
import functools

import jax
import jax.numpy as jnp
from jax import lax
from jax.experimental import pallas as pl
from jax.experimental.pallas import tpu as pltpu
from jax.sharding import PartitionSpec as P

MESH = pl.DeviceIdType.MESH
NLAT = 128
NLON = 128
SUBCYCLES = 4
EDGE_LATS = (-1, 0, 1, 14, 15, 16)
WIDE = 256
RELAYS = {1: (31, None), 4: (31, 0), 5: (31, 12), 6: (19, 10), 7: (21, 3), 8: (28, 5), 9: (26, 0), 10: (26, None)}
RELAY_TURN = {4: 1, 5: 1, 6: 1, 7: 2, 8: 1, 9: 1, 10: 2}
F32 = jnp.float32
BF16 = jnp.bfloat16


def split(values):
    high = values.astype(BF16)
    return high, (values - high.astype(F32)).astype(BF16)


def dot(a, b):
    return jnp.dot(a, b, preferred_element_type=F32)


def upwind(center, below, above, courant, from_below):
    nearby = jnp.where(from_below, below, above)
    return center - courant * (center - nearby)


def sweep_matrix(lat, lon_ref, zonal_ref, counts_ref):
    rate = lon_ref[pl.ds(lat, 1), :]
    west = jnp.broadcast_to(zonal_ref[pl.ds(lat, 1), :], (NLON, NLON)) == 1
    count = counts_ref[lat]
    row = lax.broadcasted_iota(jnp.int32, (NLON, NLON), 0)
    column = lax.broadcasted_iota(jnp.int32, (NLON, NLON), 1)
    current = jnp.where(row == column, 1.0, 0.0).astype(F32)
    for cycle in range(SUBCYCLES):
        cell_rate = jnp.where(cycle < count, rate, 0.0)
        nearby = jnp.where(
            west, pltpu.roll(current, 1, 1), pltpu.roll(current, NLON - 1, 1)
        )
        current = current - cell_rate * (current - nearby)
    return current


def kernel(
    rows_n, cols_n,
    cov, lon_hbm, lat_hbm, zonal_hbm, sign_hbm, counts_hbm,
    final, wide, col_mid, col_hi, col_lo, edge_rows,
    ext, relayed, row_mid, edge_row_mid,
    lon_ref, lat_ref, zonal_ref, sign_ref, counts_ref,
    row_rate, row_sign, row_hi, row_lo,
    load_sem, table_sem, row_send, row_recv, relay_recv, relay_send, col_send, col_recv,
):
    r, c = lax.axis_index("row"), lax.axis_index("col")
    rows, cols = cov.shape
    row_lats, col_lats = rows // NLON, cols // NLON
    halo = 2 * NLON
    inner = cols // WIDE - 3
    pieces = inner + 6
    first_row, first_col = r * row_lats, c * col_lats
    has_down, has_up = r > 0, r < rows_n - 1
    has_left, has_right = c > 0, c < cols_n - 1
    down, up = (r - 1, c), (r + 1, c)
    left, right = (r, c - 1), (r, c + 1)

    half = rows_n // 2
    below_gap, above_gap = r == half - 1, r == half
    to_below_gap, to_above_gap = (half - 1, c), (half, c)

    barrier = pltpu.get_barrier_semaphore()
    links = [(has_down, down), (has_up, up), (has_left, left), (has_right, right)]
    for relay in sorted({relay for pair in RELAYS.values() for relay in pair if relay is not None}):
        links += [
            (below_gap, (relay, c)), (above_gap, (relay, c)),
            (r == relay, to_below_gap), (r == relay, to_above_gap),
        ]
    for exists, device in links:
        @pl.when(exists)
        def _():
            pl.semaphore_signal(barrier, inc=1, device_id=device, device_id_type=MESH)

    tables = [
        pltpu.make_async_copy(source, target, table_sem.at[i])
        for i, (source, target) in enumerate((
            (lat_hbm, lat_ref), (sign_hbm, sign_ref), (lon_hbm, lon_ref),
            (zonal_hbm, zonal_ref), (counts_hbm, counts_ref),
        ))
    ]
    for table in tables:
        table.start()
    load = pltpu.make_async_copy(cov, ext.at[pl.ds(halo, rows), :], load_sem)
    load.start()

    pl.semaphore_wait(barrier, sum(exists.astype(jnp.int32) for exists, _ in links))

    def piece_columns(piece):
        if piece < 4:
            lat = (0, 1, col_lats - 2, col_lats - 1)[piece]
            return pl.ds(lat * NLON, NLON)
        if piece < 4 + inner:
            return inner_columns(piece - 4)
        return pl.ds(inner_end + (piece - 4 - inner) * NLON, NLON)

    inner_end = (inner + 1) * WIDE

    def inner_columns(chunk):
        return pl.ds(pl.multiple_of((chunk + 1) * WIDE, WIDE), WIDE)

    def to_down(piece, at):
        return pltpu.make_async_remote_copy(
            cov.at[pl.ds(0, halo), at], ext.at[pl.ds(halo + rows, halo), at],
            row_send.at[0, piece], row_recv.at[0, piece],
            device_id=down, device_id_type=MESH,
        )

    def to_up(piece, at):
        return pltpu.make_async_remote_copy(
            cov.at[pl.ds(rows - halo, halo), at], ext.at[pl.ds(0, halo), at],
            row_send.at[1, piece], row_recv.at[1, piece],
            device_id=up, device_id_type=MESH,
        )

    def to_relay(piece, at, rising):
        return pltpu.make_async_remote_copy(
            cov.at[pl.ds(rows - halo if rising else 0, halo), at], relayed.at[:, at],
            row_send.at[int(rising), piece], relay_recv.at[piece],
            device_id=(RELAYS[piece][0 if rising else 1], c), device_id_type=MESH,
        )

    def from_relay(piece, at, rising):
        return pltpu.make_async_remote_copy(
            relayed.at[:, at], ext.at[pl.ds(0 if rising else halo + rows, halo), at],
            relay_send.at[piece], row_recv.at[int(rising), piece],
            device_id=to_above_gap if rising else to_below_gap, device_id_type=MESH,
        )

    order = (0, 3, 1, 2, *range(4, pieces))
    for piece in order:
        at = piece_columns(piece)
        by_top, by_bottom = RELAYS.get(piece, (None, None))
        for relay, rising, gap, exists, direct in (
            (by_bottom, False, above_gap, has_down, to_down),
            (by_top, True, below_gap, has_up, to_up),
        ):
            if relay is None:
                @pl.when(exists)
                def _():
                    direct(piece, at).start()
            else:
                @pl.when(gap)
                def _():
                    to_relay(piece, at, rising).start()

                @pl.when(jnp.logical_and(exists, jnp.logical_not(gap)))
                def _():
                    direct(piece, at).start()

    @pl.when(jnp.logical_not(has_down))
    def _():
        ext[pl.ds(0, halo), :] = jnp.zeros((halo, cols), F32)

    @pl.when(jnp.logical_not(has_up))
    def _():
        ext[pl.ds(halo + rows, halo), :] = jnp.zeros((halo, cols), F32)

    @pl.when(jnp.logical_not(has_left))
    def _():
        wide[:, pl.ds(0, halo)] = jnp.zeros((rows, halo), F32)

    @pl.when(jnp.logical_not(has_right))
    def _():
        wide[:, pl.ds(halo + cols, halo)] = jnp.zeros((rows, halo), F32)

    def clamped(lat):
        return jnp.clip(lat, 0, NLAT - 1)

    def courant_of(lat):
        inside = jnp.logical_and(lat >= 0, lat < NLAT)
        return jnp.where(inside, lat_ref[pl.ds(clamped(lat), 1), :], 0.0)

    for table in tables:
        table.wait()

    def prepare_row(i, carry):
        lat = first_row - 1 + i
        at = clamped(lat)
        row_rate[i] = jnp.broadcast_to(courant_of(lat), (NLON, NLON)).T
        row_sign[i] = jnp.broadcast_to(
            sign_ref[pl.ds(at, 1), :].astype(F32), (NLON, NLON)
        ).T
        high, low = split(sweep_matrix(at, lon_ref, zonal_ref, counts_ref).T)
        row_hi[i] = high
        row_lo[i] = low
        return carry

    lax.fori_loop(0, row_lats + 2, prepare_row, 0, unroll=3)

    def prepare_col(i, carry):
        at = clamped(first_col - 1 + i)
        high, low = split(sweep_matrix(at, lon_ref, zonal_ref, counts_ref))
        col_hi[i] = high
        col_lo[i] = low
        return carry

    def row_chunk(piece, start, width):
        at = pl.ds(start, width)

        @pl.when(has_down)
        def _():
            to_up(piece, at).wait_recv()

        @pl.when(has_up)
        def _():
            to_down(piece, at).wait_recv()

        def across(table):
            return jnp.concatenate([table] * (width // NLON), axis=1)

        for i in range(row_lats + 2):
            below = ext[pl.ds(i * NLON, NLON), at]
            center = ext[pl.ds((i + 1) * NLON, NLON), at]
            above = ext[pl.ds((i + 2) * NLON, NLON), at]
            moved = upwind(center, below, above, across(row_rate[i]), across(row_sign[i]) == 1.0)
            high, low = split(moved)
            row_mid[i, :, pl.ds(0, width)] = (
                dot(row_hi[i], high) + (dot(row_hi[i], low) + dot(row_lo[i], high))
            )
        mids = [row_mid[i, :, pl.ds(0, width)] for i in range(row_lats + 2)]
        own = pl.ds(pl.multiple_of(halo + start, NLON), width)
        for i in range(1, row_lats + 1):
            wide[pl.ds((i - 1) * NLON, NLON), own] = upwind(
                mids[i], mids[i - 1], mids[i + 1],
                across(row_rate[i]), across(row_sign[i]) == 1.0,
            )

    def lat_columns(index):
        return pl.ds(pl.multiple_of(index * NLON, NLON), NLON)

    def col_middle(i):
        lat = first_col - 1 + i
        from_below = sign_ref[pl.ds(clamped(lat), 1), :] == 1
        moved = upwind(
            wide[:, lat_columns(i + 1)], wide[:, lat_columns(i)], wide[:, lat_columns(i + 2)],
            courant_of(lat), from_below,
        )
        high, low = split(moved)
        col_mid[:, lat_columns(i)] = (
            dot(high, col_hi[i]) + (dot(low, col_hi[i]) + dot(high, col_lo[i]))
        )

    def col_final(k):
        lat = first_col + k
        from_below = sign_ref[pl.ds(lat, 1), :] == 1
        final[:, lat_columns(k)] = upwind(
            col_mid[:, lat_columns(k + 1)], col_mid[:, lat_columns(k)],
            col_mid[:, lat_columns(k + 2)], courant_of(lat), from_below,
        )

    core = lax.rem(r, 2)

    def half_rows(late):
        part = core if late else 1 - core
        return pl.ds(pl.multiple_of(part * (rows // 2), rows // 2), rows // 2)

    def to_left(lat, late):
        at = half_rows(late)
        return pltpu.make_async_remote_copy(
            wide.at[at, pl.ds(halo + lat * NLON, NLON)],
            wide.at[at, pl.ds(halo + cols + lat * NLON, NLON)],
            col_send.at[0, 2 * lat + late], col_recv.at[0, 2 * lat + late],
            device_id=left, device_id_type=MESH,
        )

    def to_right(lat, late):
        at = half_rows(late)
        return pltpu.make_async_remote_copy(
            wide.at[at, pl.ds(cols + lat * NLON, NLON)],
            wide.at[at, pl.ds(lat * NLON, NLON)],
            col_send.at[1, 2 * lat + late], col_recv.at[1, 2 * lat + late],
            device_id=right, device_id_type=MESH,
        )

    def edge_half(piece, late):
        start = (0, 1, col_lats - 2, col_lats - 1)[piece] * NLON
        at = pl.ds(start, NLON)

        @pl.when(jnp.logical_and(core == late, has_up))
        def _():
            to_down(piece, at).wait_recv()

        @pl.when(jnp.logical_and(core != late, has_down))
        def _():
            to_up(piece, at).wait_recv()

        def lat_rows(index):
            return pl.ds(pl.multiple_of(index * NLON, NLON), NLON)

        upper = 1 - core
        first = 4 - 4 * upper if late else 2 * upper
        for step in range(2 if late else 4):
            i = first + step
            moved = upwind(
                ext[lat_rows(i + 1), at], ext[lat_rows(i), at], ext[lat_rows(i + 2), at],
                row_rate[i], row_sign[i] == 1.0,
            )
            high, low = split(moved)
            edge_row_mid[piece, i] = (
                dot(row_hi[i], high) + (dot(row_hi[i], low) + dot(row_lo[i], high))
            )
        first = 2 - 2 * upper if late else 2 * upper
        for step in range(1, 3):
            i = first + step
            wide[lat_rows(i - 1), pl.ds(halo + start, NLON)] = upwind(
                edge_row_mid[piece, i], edge_row_mid[piece, i - 1], edge_row_mid[piece, i + 1],
                row_rate[i], row_sign[i] == 1.0,
            )
        if piece < 2:
            @pl.when(has_left)
            def _():
                to_left(piece, late).start()
        else:
            @pl.when(has_right)
            def _():
                to_right(piece - 2, late).start()

    def pass_on(piece):
        at = piece_columns(piece)
        for relay, rising in zip(RELAYS[piece], (True, False)):
            if relay is None:
                continue

            @pl.when(r == relay)
            def _():
                to_relay(piece, at, rising).wait_recv()
                from_relay(piece, at, rising).start()

    load.wait()
    for late in range(2):
        for piece in (0, 3, 1, 2):
            if late and piece in RELAYS:
                pass_on(piece)
            edge_half(piece, late)

    lax.fori_loop(0, col_lats + 2, prepare_col, 0, unroll=3)

    def interior(chunk, carry):
        for turn in sorted(set(RELAY_TURN.values())):
            @pl.when(chunk == turn)
            def _():
                for piece in RELAY_TURN:
                    if RELAY_TURN[piece] == turn:
                        pass_on(piece)

        row_chunk(4 + chunk, pl.multiple_of((chunk + 1) * WIDE, WIDE), WIDE)
        col_middle(2 * chunk + 2)
        col_middle(2 * chunk + 3)

        @pl.when(chunk > 0)
        def _():
            col_final(2 * chunk)
            col_final(2 * chunk + 1)

        return carry

    lax.fori_loop(0, inner, interior, 0)

    for i, lat in enumerate(EDGE_LATS):
        edge_rows[pl.ds(i, 1), :] = courant_of(first_col + lat)
        edge_rows[pl.ds(8 + i, 1), :] = sign_ref[
            pl.ds(clamped(first_col + lat), 1), :
        ].astype(F32)

    row_chunk(pieces - 2, inner_end, NLON)
    col_middle(col_lats - 4)
    col_final(col_lats - 6)
    row_chunk(pieces - 1, inner_end + NLON, NLON)
    for i in range(col_lats - 3, col_lats):
        col_middle(i)
    for k in range(col_lats - 5, col_lats - 2):
        col_final(k)

    @pl.when(has_right)
    def _():
        for lat in range(2):
            for late in range(2):
                to_left(lat, late).wait_recv()

    @pl.when(has_left)
    def _():
        for lat in range(2):
            for late in range(2):
                to_right(lat, late).wait_recv()

    for piece in order:
        at = piece_columns(piece)

        @pl.when(has_down)
        def _():
            to_down(piece, at).wait_send()

        @pl.when(has_up)
        def _():
            to_up(piece, at).wait_send()

        if piece in RELAYS:
            for relay, rising in zip(RELAYS[piece], (True, False)):
                if relay is None:
                    continue

                @pl.when(r == relay)
                def _():
                    from_relay(piece, at, rising).wait_send()

    for lat in range(2):
        for late in range(2):
            @pl.when(has_left)
            def _():
                to_left(lat, late).wait_send()

            @pl.when(has_right)
            def _():
                to_right(lat, late).wait_send()


def finish(
    final, wide, col_mid, col_hi, col_lo, edge_rows, out, edge_mid, edge_final, sems
):
    rows, cols = final.shape
    col_lats = cols // NLON
    edge = 2 * NLON
    inner = pl.ds(edge, cols - 2 * edge)
    stores = [pltpu.make_async_copy(final.at[:, inner], out.at[:, inner], sems.at[0])]
    stores[0].start()

    def lat_columns(index):
        return pl.ds(index * NLON, NLON)

    def row_of(lat):
        at = EDGE_LATS.index(lat)
        return edge_rows[pl.ds(at, 1), :], edge_rows[pl.ds(8 + at, 1), :] == 1.0

    def middle(lat):
        moved = upwind(
            wide[:, lat_columns(lat + 2)], wide[:, lat_columns(lat + 1)],
            wide[:, lat_columns(lat + 3)], *row_of(lat),
        )
        high, low = split(moved)
        i = lat + 1
        return dot(high, col_hi[i]) + (dot(low, col_hi[i]) + dot(high, col_lo[i]))

    for side, (outer, near) in enumerate((((-1, 0), (1, 2)), ((col_lats, col_lats - 1), (col_lats - 2, col_lats - 3)))):
        for at, lat in enumerate(outer):
            edge_mid[side, at] = middle(lat)
        mids = {lat: edge_mid[side, at] for at, lat in enumerate(outer)}
        mids |= {lat: col_mid[:, lat_columns(lat + 1)] for lat in near}
        first = 0 if side == 0 else cols - edge
        for lat in (outer[1], near[0]):
            place = lat * NLON - first
            edge_final[side, :, pl.ds(place, NLON)] = upwind(
                mids[lat], mids[lat - 1], mids[lat + 1], *row_of(lat)
            )
        store = pltpu.make_async_copy(
            edge_final.at[side], out.at[:, pl.ds(first, edge)], sems.at[1 + side]
        )
        store.start()
        stores.append(store)
    for store in stores:
        store.wait()


def solution(mesh):
    rows_n, cols_n = mesh.shape["row"], mesh.shape["col"]

    def per_device(covariance, lon_courant, lat_courant, zonal_upwind_sign, lat_sign, cycle_counts):
        rows, cols = covariance.shape
        row_lats, col_lats = rows // NLON, cols // NLON
        pieces = cols // WIDE + 3
        hbm = pl.BlockSpec(memory_space=pltpu.HBM)
        vmem = pl.BlockSpec(memory_space=pltpu.VMEM)
        parts = pl.pallas_call(
            functools.partial(kernel, rows_n, cols_n),
            out_shape=[
                jax.ShapeDtypeStruct((rows, cols), F32),
                jax.ShapeDtypeStruct((rows, cols + 4 * NLON), F32),
                jax.ShapeDtypeStruct((rows, cols + 2 * NLON), F32),
                jax.ShapeDtypeStruct((col_lats + 2, NLON, NLON), BF16),
                jax.ShapeDtypeStruct((col_lats + 2, NLON, NLON), BF16),
                jax.ShapeDtypeStruct((16, NLON), F32),
            ],
            in_specs=[hbm] * 6,
            out_specs=[vmem] * 6,
            scratch_shapes=[
                pltpu.VMEM((rows + 4 * NLON, cols), F32),
                pltpu.VMEM((2 * NLON, cols), F32),
                pltpu.VMEM((row_lats + 2, NLON, WIDE), F32),
                pltpu.VMEM((4, row_lats + 2, NLON, NLON), F32),
                pltpu.VMEM((NLAT, NLON), F32),
                pltpu.VMEM((NLAT, NLON), F32),
                pltpu.VMEM((NLAT, NLON), jnp.int32),
                pltpu.VMEM((NLAT, NLON), jnp.int32),
                pltpu.SMEM((NLAT,), jnp.int32),
                pltpu.VMEM((row_lats + 2, NLON, NLON), F32),
                pltpu.VMEM((row_lats + 2, NLON, NLON), F32),
                pltpu.VMEM((row_lats + 2, NLON, NLON), BF16),
                pltpu.VMEM((row_lats + 2, NLON, NLON), BF16),
                pltpu.SemaphoreType.DMA,
                pltpu.SemaphoreType.DMA((5,)),
                pltpu.SemaphoreType.DMA((2, pieces)),
                pltpu.SemaphoreType.DMA((2, pieces)),
                pltpu.SemaphoreType.DMA((pieces,)),
                pltpu.SemaphoreType.DMA((pieces,)),
                pltpu.SemaphoreType.DMA((2, 4)),
                pltpu.SemaphoreType.DMA((2, 4)),
            ],
            name="forecast",
            compiler_params=pltpu.CompilerParams(
                collective_id=0, has_side_effects=True, vmem_limit_bytes=36 * 2**20
            ),
        )(*[pltpu.with_memory_space_constraint(a, pltpu.HBM) for a in (covariance, lon_courant, lat_courant, zonal_upwind_sign, lat_sign, cycle_counts)])
        return pl.pallas_call(
            finish,
            out_shape=jax.ShapeDtypeStruct((rows, cols), F32),
            in_specs=[vmem] * 6,
            out_specs=hbm,
            scratch_shapes=[
                pltpu.VMEM((2, 2, rows, NLON), F32),
                pltpu.VMEM((2, rows, 2 * NLON), F32),
                pltpu.SemaphoreType.DMA((3,)),
            ],
            name="finish",
            compiler_params=pltpu.CompilerParams(vmem_limit_bytes=36 * 2**20),
        )(*parts)

    placed = (P("row", "col"), P(), P(), P(), P(), P())
    return jax.shard_map(
        per_device, mesh=mesh, in_specs=placed, out_specs=P("row", "col"), check_vma=False
    )
```

```python
import functools

import jax
import jax.numpy as jnp
from jax import lax
from jax.experimental import pallas as pl
from jax.experimental.pallas import tpu as pltpu
from jax.sharding import PartitionSpec as P

MESH = pl.DeviceIdType.MESH
NLAT = 128
NLON = 128
SUBCYCLES = 4
EDGE_LATS = (-1, 0, 1, 14, 15, 16)
WIDE = 256
RELAYS = {1: (31, None), 4: (31, 0), 5: (31, 12), 6: (19, 10), 7: (21, 3), 8: (28, 5), 9: (26, 0), 10: (26, None)}
RELAY_TURN = {4: 1, 5: 1, 6: 1, 7: 2, 8: 1, 9: 1, 10: 2}
F32 = jnp.float32
BF16 = jnp.bfloat16


def split(values):
    high = values.astype(BF16)
    return high, (values - high.astype(F32)).astype(BF16)


def dot(a, b):
    return jnp.dot(a, b, preferred_element_type=F32)


def upwind(center, below, above, courant, from_below):
    nearby = jnp.where(from_below, below, above)
    return center - courant * (center - nearby)


def sweep_matrix(lat, lon_ref, zonal_ref, counts_ref):
    rate = lon_ref[pl.ds(lat, 1), :]
    west = jnp.broadcast_to(zonal_ref[pl.ds(lat, 1), :], (NLON, NLON)) == 1
    count = counts_ref[lat]
    row = lax.broadcasted_iota(jnp.int32, (NLON, NLON), 0)
    column = lax.broadcasted_iota(jnp.int32, (NLON, NLON), 1)
    current = jnp.where(row == column, 1.0, 0.0).astype(F32)
    for cycle in range(SUBCYCLES):
        cell_rate = jnp.where(cycle < count, rate, 0.0)
        nearby = jnp.where(
            west, pltpu.roll(current, 1, 1), pltpu.roll(current, NLON - 1, 1)
        )
        current = current - cell_rate * (current - nearby)
    return current


def kernel(
    rows_n, cols_n,
    cov, lon_hbm, lat_hbm, zonal_hbm, sign_hbm, counts_hbm,
    final, wide, col_mid, col_hi, col_lo, edge_rows,
    ext, relayed, row_mid, edge_row_mid,
    lon_ref, lat_ref, zonal_ref, sign_ref, counts_ref,
    row_rate, row_sign, row_hi, row_lo,
    load_sem, table_sem, row_send, row_recv, relay_recv, relay_send, col_send, col_recv,
):
    r, c = lax.axis_index("row"), lax.axis_index("col")
    rows, cols = cov.shape
    row_lats, col_lats = rows // NLON, cols // NLON
    halo = 2 * NLON
    inner = cols // WIDE - 3
    pieces = inner + 6
    first_row, first_col = r * row_lats, c * col_lats
    has_down, has_up = r > 0, r < rows_n - 1
    has_left, has_right = c > 0, c < cols_n - 1
    down, up = (r - 1, c), (r + 1, c)
    left, right = (r, c - 1), (r, c + 1)

    half = rows_n // 2
    below_gap, above_gap = r == half - 1, r == half
    to_below_gap, to_above_gap = (half - 1, c), (half, c)

    barrier = pltpu.get_barrier_semaphore()
    links = [(has_down, down), (has_up, up), (has_left, left), (has_right, right)]
    for relay in sorted({relay for pair in RELAYS.values() for relay in pair if relay is not None}):
        links += [
            (below_gap, (relay, c)), (above_gap, (relay, c)),
            (r == relay, to_below_gap), (r == relay, to_above_gap),
        ]
    def greet(pairs):
        for exists, device in pairs:
            @pl.when(exists)
            def _():
                pl.semaphore_signal(barrier, inc=1, device_id=device, device_id_type=MESH)

    near = 4
    relaying = functools.reduce(jnp.logical_or, [exists for exists, _ in links[near:]])

    @pl.when(relaying)
    def _():
        greet(links[near:])

    greet(links[:near])

    tables = [
        pltpu.make_async_copy(source, target, table_sem.at[i])
        for i, (source, target) in enumerate((
            (lat_hbm, lat_ref), (sign_hbm, sign_ref), (lon_hbm, lon_ref),
            (zonal_hbm, zonal_ref), (counts_hbm, counts_ref),
        ))
    ]
    for table in tables:
        table.start()
    load = pltpu.make_async_copy(cov, ext.at[pl.ds(halo, rows), :], load_sem)
    load.start()

    pl.semaphore_wait(barrier, sum(exists.astype(jnp.int32) for exists, _ in links))

    def piece_columns(piece):
        if piece < 4:
            lat = (0, 1, col_lats - 2, col_lats - 1)[piece]
            return pl.ds(lat * NLON, NLON)
        if piece < 4 + inner:
            return inner_columns(piece - 4)
        return pl.ds(inner_end + (piece - 4 - inner) * NLON, NLON)

    inner_end = (inner + 1) * WIDE

    def inner_columns(chunk):
        return pl.ds(pl.multiple_of((chunk + 1) * WIDE, WIDE), WIDE)

    def to_down(piece, at):
        return pltpu.make_async_remote_copy(
            cov.at[pl.ds(0, halo), at], ext.at[pl.ds(halo + rows, halo), at],
            row_send.at[0, piece], row_recv.at[0, piece],
            device_id=down, device_id_type=MESH,
        )

    def to_up(piece, at):
        return pltpu.make_async_remote_copy(
            cov.at[pl.ds(rows - halo, halo), at], ext.at[pl.ds(0, halo), at],
            row_send.at[1, piece], row_recv.at[1, piece],
            device_id=up, device_id_type=MESH,
        )

    def to_relay(piece, at, rising):
        return pltpu.make_async_remote_copy(
            cov.at[pl.ds(rows - halo if rising else 0, halo), at], relayed.at[:, at],
            row_send.at[int(rising), piece], relay_recv.at[piece],
            device_id=(RELAYS[piece][0 if rising else 1], c), device_id_type=MESH,
        )

    def from_relay(piece, at, rising):
        return pltpu.make_async_remote_copy(
            relayed.at[:, at], ext.at[pl.ds(0 if rising else halo + rows, halo), at],
            relay_send.at[piece], row_recv.at[int(rising), piece],
            device_id=to_above_gap if rising else to_below_gap, device_id_type=MESH,
        )

    order = (0, 3, 1, 2, *range(4, pieces))
    for piece in order:
        at = piece_columns(piece)
        by_top, by_bottom = RELAYS.get(piece, (None, None))
        for relay, rising, gap, exists, direct in (
            (by_bottom, False, above_gap, has_down, to_down),
            (by_top, True, below_gap, has_up, to_up),
        ):
            if relay is None:
                @pl.when(exists)
                def _():
                    direct(piece, at).start()
            else:
                @pl.when(gap)
                def _():
                    to_relay(piece, at, rising).start()

                @pl.when(jnp.logical_and(exists, jnp.logical_not(gap)))
                def _():
                    direct(piece, at).start()

    @pl.when(jnp.logical_not(has_down))
    def _():
        ext[pl.ds(0, halo), :] = jnp.zeros((halo, cols), F32)

    @pl.when(jnp.logical_not(has_up))
    def _():
        ext[pl.ds(halo + rows, halo), :] = jnp.zeros((halo, cols), F32)

    @pl.when(jnp.logical_not(has_left))
    def _():
        wide[:, pl.ds(0, halo)] = jnp.zeros((rows, halo), F32)

    @pl.when(jnp.logical_not(has_right))
    def _():
        wide[:, pl.ds(halo + cols, halo)] = jnp.zeros((rows, halo), F32)

    def clamped(lat):
        return jnp.clip(lat, 0, NLAT - 1)

    def courant_of(lat):
        inside = jnp.logical_and(lat >= 0, lat < NLAT)
        return jnp.where(inside, lat_ref[pl.ds(clamped(lat), 1), :], 0.0)

    for table in tables:
        table.wait()

    def prepare_row(i, carry):
        lat = first_row - 1 + i
        at = clamped(lat)
        row_rate[i] = jnp.broadcast_to(courant_of(lat), (NLON, NLON)).T
        row_sign[i] = jnp.broadcast_to(
            sign_ref[pl.ds(at, 1), :].astype(F32), (NLON, NLON)
        ).T
        high, low = split(sweep_matrix(at, lon_ref, zonal_ref, counts_ref).T)
        row_hi[i] = high
        row_lo[i] = low
        return carry

    lax.fori_loop(0, row_lats + 2, prepare_row, 0, unroll=3)

    def prepare_col(i, carry):
        at = clamped(first_col - 1 + i)
        high, low = split(sweep_matrix(at, lon_ref, zonal_ref, counts_ref))
        col_hi[i] = high
        col_lo[i] = low
        return carry

    def row_chunk(piece, start, width):
        at = pl.ds(start, width)

        @pl.when(has_down)
        def _():
            to_up(piece, at).wait_recv()

        @pl.when(has_up)
        def _():
            to_down(piece, at).wait_recv()

        def across(table):
            return jnp.concatenate([table] * (width // NLON), axis=1)

        for i in range(row_lats + 2):
            below = ext[pl.ds(i * NLON, NLON), at]
            center = ext[pl.ds((i + 1) * NLON, NLON), at]
            above = ext[pl.ds((i + 2) * NLON, NLON), at]
            moved = upwind(center, below, above, across(row_rate[i]), across(row_sign[i]) == 1.0)
            high, low = split(moved)
            row_mid[i, :, pl.ds(0, width)] = (
                dot(row_hi[i], high) + (dot(row_hi[i], low) + dot(row_lo[i], high))
            )
        mids = [row_mid[i, :, pl.ds(0, width)] for i in range(row_lats + 2)]
        own = pl.ds(pl.multiple_of(halo + start, NLON), width)
        for i in range(1, row_lats + 1):
            wide[pl.ds((i - 1) * NLON, NLON), own] = upwind(
                mids[i], mids[i - 1], mids[i + 1],
                across(row_rate[i]), across(row_sign[i]) == 1.0,
            )

    def lat_columns(index):
        return pl.ds(pl.multiple_of(index * NLON, NLON), NLON)

    def col_middle(i):
        lat = first_col - 1 + i
        from_below = sign_ref[pl.ds(clamped(lat), 1), :] == 1
        moved = upwind(
            wide[:, lat_columns(i + 1)], wide[:, lat_columns(i)], wide[:, lat_columns(i + 2)],
            courant_of(lat), from_below,
        )
        high, low = split(moved)
        col_mid[:, lat_columns(i)] = (
            dot(high, col_hi[i]) + (dot(low, col_hi[i]) + dot(high, col_lo[i]))
        )

    def col_final(k):
        lat = first_col + k
        from_below = sign_ref[pl.ds(lat, 1), :] == 1
        final[:, lat_columns(k)] = upwind(
            col_mid[:, lat_columns(k + 1)], col_mid[:, lat_columns(k)],
            col_mid[:, lat_columns(k + 2)], courant_of(lat), from_below,
        )

    core = lax.rem(r, 2)

    def half_rows(late):
        part = core if late else 1 - core
        return pl.ds(pl.multiple_of(part * (rows // 2), rows // 2), rows // 2)

    def to_left(lat, late):
        at = half_rows(late)
        return pltpu.make_async_remote_copy(
            wide.at[at, pl.ds(halo + lat * NLON, NLON)],
            wide.at[at, pl.ds(halo + cols + lat * NLON, NLON)],
            col_send.at[0, 2 * lat + late], col_recv.at[0, 2 * lat + late],
            device_id=left, device_id_type=MESH,
        )

    def to_right(lat, late):
        at = half_rows(late)
        return pltpu.make_async_remote_copy(
            wide.at[at, pl.ds(cols + lat * NLON, NLON)],
            wide.at[at, pl.ds(lat * NLON, NLON)],
            col_send.at[1, 2 * lat + late], col_recv.at[1, 2 * lat + late],
            device_id=right, device_id_type=MESH,
        )

    def edge_half(piece, late):
        start = (0, 1, col_lats - 2, col_lats - 1)[piece] * NLON
        at = pl.ds(start, NLON)

        @pl.when(jnp.logical_and(core == late, has_up))
        def _():
            to_down(piece, at).wait_recv()

        @pl.when(jnp.logical_and(core != late, has_down))
        def _():
            to_up(piece, at).wait_recv()

        def lat_rows(index):
            return pl.ds(pl.multiple_of(index * NLON, NLON), NLON)

        upper = 1 - core
        first = 4 - 4 * upper if late else 2 * upper
        for step in range(2 if late else 4):
            i = first + step
            moved = upwind(
                ext[lat_rows(i + 1), at], ext[lat_rows(i), at], ext[lat_rows(i + 2), at],
                row_rate[i], row_sign[i] == 1.0,
            )
            high, low = split(moved)
            edge_row_mid[piece, i] = (
                dot(row_hi[i], high) + (dot(row_hi[i], low) + dot(row_lo[i], high))
            )
        first = 2 - 2 * upper if late else 2 * upper
        for step in range(1, 3):
            i = first + step
            wide[lat_rows(i - 1), pl.ds(halo + start, NLON)] = upwind(
                edge_row_mid[piece, i], edge_row_mid[piece, i - 1], edge_row_mid[piece, i + 1],
                row_rate[i], row_sign[i] == 1.0,
            )
        if piece < 2:
            @pl.when(has_left)
            def _():
                to_left(piece, late).start()
        else:
            @pl.when(has_right)
            def _():
                to_right(piece - 2, late).start()

    def pass_on(piece):
        at = piece_columns(piece)
        for relay, rising in zip(RELAYS[piece], (True, False)):
            if relay is None:
                continue

            @pl.when(r == relay)
            def _():
                to_relay(piece, at, rising).wait_recv()
                from_relay(piece, at, rising).start()

    load.wait()
    for late in range(2):
        for piece in (0, 3, 1, 2):
            if late and piece in RELAYS:
                pass_on(piece)
            edge_half(piece, late)

    lax.fori_loop(0, col_lats + 2, prepare_col, 0, unroll=3)

    def interior(chunk, carry):
        for turn in sorted(set(RELAY_TURN.values())):
            @pl.when(chunk == turn)
            def _():
                for piece in RELAY_TURN:
                    if RELAY_TURN[piece] == turn:
                        pass_on(piece)

        row_chunk(4 + chunk, pl.multiple_of((chunk + 1) * WIDE, WIDE), WIDE)
        col_middle(2 * chunk + 2)
        col_middle(2 * chunk + 3)

        @pl.when(chunk > 0)
        def _():
            col_final(2 * chunk)
            col_final(2 * chunk + 1)

        return carry

    lax.fori_loop(0, inner, interior, 0)

    for i, lat in enumerate(EDGE_LATS):
        edge_rows[pl.ds(i, 1), :] = courant_of(first_col + lat)
        edge_rows[pl.ds(8 + i, 1), :] = sign_ref[
            pl.ds(clamped(first_col + lat), 1), :
        ].astype(F32)

    row_chunk(pieces - 2, inner_end, NLON)
    col_middle(col_lats - 4)
    col_final(col_lats - 6)
    row_chunk(pieces - 1, inner_end + NLON, NLON)
    for i in range(col_lats - 3, col_lats):
        col_middle(i)
    for k in range(col_lats - 5, col_lats - 2):
        col_final(k)

    @pl.when(has_right)
    def _():
        for lat in range(2):
            for late in range(2):
                to_left(lat, late).wait_recv()

    @pl.when(has_left)
    def _():
        for lat in range(2):
            for late in range(2):
                to_right(lat, late).wait_recv()

    for piece in order:
        at = piece_columns(piece)

        @pl.when(has_down)
        def _():
            to_down(piece, at).wait_send()

        @pl.when(has_up)
        def _():
            to_up(piece, at).wait_send()

        if piece in RELAYS:
            for relay, rising in zip(RELAYS[piece], (True, False)):
                if relay is None:
                    continue

                @pl.when(r == relay)
                def _():
                    from_relay(piece, at, rising).wait_send()

    for lat in range(2):
        for late in range(2):
            @pl.when(has_left)
            def _():
                to_left(lat, late).wait_send()

            @pl.when(has_right)
            def _():
                to_right(lat, late).wait_send()


def finish(
    final, wide, col_mid, col_hi, col_lo, edge_rows, out, edge_mid, edge_final, sems
):
    rows, cols = final.shape
    col_lats = cols // NLON
    edge = 2 * NLON
    inner = pl.ds(edge, cols - 2 * edge)
    stores = [pltpu.make_async_copy(final.at[:, inner], out.at[:, inner], sems.at[0])]
    stores[0].start()

    def lat_columns(index):
        return pl.ds(index * NLON, NLON)

    def row_of(lat):
        at = EDGE_LATS.index(lat)
        return edge_rows[pl.ds(at, 1), :], edge_rows[pl.ds(8 + at, 1), :] == 1.0

    def middle(lat):
        moved = upwind(
            wide[:, lat_columns(lat + 2)], wide[:, lat_columns(lat + 1)],
            wide[:, lat_columns(lat + 3)], *row_of(lat),
        )
        high, low = split(moved)
        i = lat + 1
        return dot(high, col_hi[i]) + (dot(low, col_hi[i]) + dot(high, col_lo[i]))

    for side, (outer, near) in enumerate((((-1, 0), (1, 2)), ((col_lats, col_lats - 1), (col_lats - 2, col_lats - 3)))):
        for at, lat in enumerate(outer):
            edge_mid[side, at] = middle(lat)
        mids = {lat: edge_mid[side, at] for at, lat in enumerate(outer)}
        mids |= {lat: col_mid[:, lat_columns(lat + 1)] for lat in near}
        first = 0 if side == 0 else cols - edge
        for lat in (outer[1], near[0]):
            place = lat * NLON - first
            edge_final[side, :, pl.ds(place, NLON)] = upwind(
                mids[lat], mids[lat - 1], mids[lat + 1], *row_of(lat)
            )
        store = pltpu.make_async_copy(
            edge_final.at[side], out.at[:, pl.ds(first, edge)], sems.at[1 + side]
        )
        store.start()
        stores.append(store)
    for store in stores:
        store.wait()


def solution(mesh):
    rows_n, cols_n = mesh.shape["row"], mesh.shape["col"]

    def per_device(covariance, lon_courant, lat_courant, zonal_upwind_sign, lat_sign, cycle_counts):
        rows, cols = covariance.shape
        row_lats, col_lats = rows // NLON, cols // NLON
        pieces = cols // WIDE + 3
        hbm = pl.BlockSpec(memory_space=pltpu.HBM)
        vmem = pl.BlockSpec(memory_space=pltpu.VMEM)
        parts = pl.pallas_call(
            functools.partial(kernel, rows_n, cols_n),
            out_shape=[
                jax.ShapeDtypeStruct((rows, cols), F32),
                jax.ShapeDtypeStruct((rows, cols + 4 * NLON), F32),
                jax.ShapeDtypeStruct((rows, cols + 2 * NLON), F32),
                jax.ShapeDtypeStruct((col_lats + 2, NLON, NLON), BF16),
                jax.ShapeDtypeStruct((col_lats + 2, NLON, NLON), BF16),
                jax.ShapeDtypeStruct((16, NLON), F32),
            ],
            in_specs=[hbm] * 6,
            out_specs=[vmem] * 6,
            scratch_shapes=[
                pltpu.VMEM((rows + 4 * NLON, cols), F32),
                pltpu.VMEM((2 * NLON, cols), F32),
                pltpu.VMEM((row_lats + 2, NLON, WIDE), F32),
                pltpu.VMEM((4, row_lats + 2, NLON, NLON), F32),
                pltpu.VMEM((NLAT, NLON), F32),
                pltpu.VMEM((NLAT, NLON), F32),
                pltpu.VMEM((NLAT, NLON), jnp.int32),
                pltpu.VMEM((NLAT, NLON), jnp.int32),
                pltpu.SMEM((NLAT,), jnp.int32),
                pltpu.VMEM((row_lats + 2, NLON, NLON), F32),
                pltpu.VMEM((row_lats + 2, NLON, NLON), F32),
                pltpu.VMEM((row_lats + 2, NLON, NLON), BF16),
                pltpu.VMEM((row_lats + 2, NLON, NLON), BF16),
                pltpu.SemaphoreType.DMA,
                pltpu.SemaphoreType.DMA((5,)),
                pltpu.SemaphoreType.DMA((2, pieces)),
                pltpu.SemaphoreType.DMA((2, pieces)),
                pltpu.SemaphoreType.DMA((pieces,)),
                pltpu.SemaphoreType.DMA((pieces,)),
                pltpu.SemaphoreType.DMA((2, 4)),
                pltpu.SemaphoreType.DMA((2, 4)),
            ],
            name="forecast",
            compiler_params=pltpu.CompilerParams(
                collective_id=0, has_side_effects=True, vmem_limit_bytes=36 * 2**20
            ),
        )(*[pltpu.with_memory_space_constraint(a, pltpu.HBM) for a in (covariance, lon_courant, lat_courant, zonal_upwind_sign, lat_sign, cycle_counts)])
        return pl.pallas_call(
            finish,
            out_shape=jax.ShapeDtypeStruct((rows, cols), F32),
            in_specs=[vmem] * 6,
            out_specs=hbm,
            scratch_shapes=[
                pltpu.VMEM((2, 2, rows, NLON), F32),
                pltpu.VMEM((2, rows, 2 * NLON), F32),
                pltpu.SemaphoreType.DMA((3,)),
            ],
            name="finish",
            compiler_params=pltpu.CompilerParams(vmem_limit_bytes=36 * 2**20),
        )(*parts)

    placed = (P("row", "col"), P(), P(), P(), P(), P())
    return jax.shard_map(
        per_device, mesh=mesh, in_specs=placed, out_specs=P("row", "col"), check_vma=False
    )
```

```python
import functools

import jax
import jax.numpy as jnp
from jax import lax
from jax.experimental import pallas as pl
from jax.experimental.pallas import tpu as pltpu
from jax.sharding import PartitionSpec as P

MESH = pl.DeviceIdType.MESH
NLAT = 128
NLON = 128
SUBCYCLES = 4
EDGE_LATS = (-1, 0, 1, 14, 15, 16)
WIDE = 256
RELAYS = {1: (31, None), 4: (31, 0), 5: (31, 12), 6: (19, 10), 7: (21, 3), 8: (28, 5), 9: (26, 0), 10: (26, None)}
RELAY_TURN = {4: 1, 5: 1, 6: 1, 7: 2, 8: 1, 9: 1, 10: 2}
F32 = jnp.float32
BF16 = jnp.bfloat16


def split(values):
    high = values.astype(BF16)
    return high, (values - high.astype(F32)).astype(BF16)


def dot(a, b):
    return jnp.dot(a, b, preferred_element_type=F32)


def upwind(center, below, above, courant, from_below):
    nearby = jnp.where(from_below, below, above)
    return center - courant * (center - nearby)


def sweep_matrix(lat, lon_ref, zonal_ref, counts_ref):
    rate = lon_ref[pl.ds(lat, 1), :]
    west = jnp.broadcast_to(zonal_ref[pl.ds(lat, 1), :], (NLON, NLON)) == 1
    count = counts_ref[lat]
    row = lax.broadcasted_iota(jnp.int32, (NLON, NLON), 0)
    column = lax.broadcasted_iota(jnp.int32, (NLON, NLON), 1)
    current = jnp.where(row == column, 1.0, 0.0).astype(F32)
    for cycle in range(SUBCYCLES):
        cell_rate = jnp.where(cycle < count, rate, 0.0)
        nearby = jnp.where(
            west, pltpu.roll(current, 1, 1), pltpu.roll(current, NLON - 1, 1)
        )
        current = current - cell_rate * (current - nearby)
    return current


def kernel(
    rows_n, cols_n,
    cov, lon_hbm, lat_hbm, zonal_hbm, sign_hbm, counts_hbm,
    final, wide, col_mid, col_hi, col_lo, edge_rows,
    ext, relayed, row_mid, edge_row_mid,
    lon_ref, lat_ref, zonal_ref, sign_ref, counts_ref,
    row_rate, row_sign, row_hi, row_lo,
    load_sem, table_sem, row_send, row_recv, relay_recv, relay_send, col_send, col_recv,
):
    r, c = lax.axis_index("row"), lax.axis_index("col")
    rows, cols = cov.shape
    row_lats, col_lats = rows // NLON, cols // NLON
    halo = 2 * NLON
    inner = cols // WIDE - 3
    pieces = inner + 6
    first_row, first_col = r * row_lats, c * col_lats
    has_down, has_up = r > 0, r < rows_n - 1
    has_left, has_right = c > 0, c < cols_n - 1
    down, up = (r - 1, c), (r + 1, c)
    left, right = (r, c - 1), (r, c + 1)

    half = rows_n // 2
    below_gap, above_gap = r == half - 1, r == half
    to_below_gap, to_above_gap = (half - 1, c), (half, c)

    barrier = pltpu.get_barrier_semaphore()
    links = [(has_down, down), (has_up, up), (has_left, left), (has_right, right)]
    for relay in sorted({relay for pair in RELAYS.values() for relay in pair if relay is not None}):
        links += [
            (below_gap, (relay, c)), (above_gap, (relay, c)),
            (r == relay, to_below_gap), (r == relay, to_above_gap),
        ]
    def greet(pairs):
        for exists, device in pairs:
            @pl.when(exists)
            def _():
                pl.semaphore_signal(barrier, inc=1, device_id=device, device_id_type=MESH)

    near = 4
    relaying = functools.reduce(jnp.logical_or, [exists for exists, _ in links[near:]])

    @pl.when(relaying)
    def _():
        greet(links[near:])

    greet(links[:near])

    tables = [
        pltpu.make_async_copy(source, target, table_sem.at[i])
        for i, (source, target) in enumerate((
            (lat_hbm, lat_ref), (sign_hbm, sign_ref), (lon_hbm, lon_ref),
            (zonal_hbm, zonal_ref), (counts_hbm, counts_ref),
        ))
    ]
    for table in tables:
        table.start()
    load = pltpu.make_async_copy(cov, ext.at[pl.ds(halo, rows), :], load_sem)
    load.start()

    pl.semaphore_wait(barrier, sum(exists.astype(jnp.int32) for exists, _ in links))

    def piece_columns(piece):
        if piece < 4:
            lat = (0, 1, col_lats - 2, col_lats - 1)[piece]
            return pl.ds(lat * NLON, NLON)
        if piece < 4 + inner:
            return inner_columns(piece - 4)
        return pl.ds(inner_end + (piece - 4 - inner) * NLON, NLON)

    inner_end = (inner + 1) * WIDE

    def inner_columns(chunk):
        return pl.ds(pl.multiple_of((chunk + 1) * WIDE, WIDE), WIDE)

    def to_down(piece, at):
        return pltpu.make_async_remote_copy(
            cov.at[pl.ds(0, halo), at], ext.at[pl.ds(halo + rows, halo), at],
            row_send.at[0, piece], row_recv.at[0, piece],
            device_id=down, device_id_type=MESH,
        )

    def to_up(piece, at):
        return pltpu.make_async_remote_copy(
            cov.at[pl.ds(rows - halo, halo), at], ext.at[pl.ds(0, halo), at],
            row_send.at[1, piece], row_recv.at[1, piece],
            device_id=up, device_id_type=MESH,
        )

    def to_relay(piece, at, rising):
        return pltpu.make_async_remote_copy(
            cov.at[pl.ds(rows - halo if rising else 0, halo), at], relayed.at[:, at],
            row_send.at[int(rising), piece], relay_recv.at[piece],
            device_id=(RELAYS[piece][0 if rising else 1], c), device_id_type=MESH,
        )

    def from_relay(piece, at, rising):
        return pltpu.make_async_remote_copy(
            relayed.at[:, at], ext.at[pl.ds(0 if rising else halo + rows, halo), at],
            relay_send.at[piece], row_recv.at[int(rising), piece],
            device_id=to_above_gap if rising else to_below_gap, device_id_type=MESH,
        )

    order = (0, 3, 1, 2, *range(4, pieces))
    def send_piece(piece):
        at = piece_columns(piece)
        by_top, by_bottom = RELAYS.get(piece, (None, None))
        for relay, rising, gap, exists, direct in (
            (by_bottom, False, above_gap, has_down, to_down),
            (by_top, True, below_gap, has_up, to_up),
        ):
            if relay is None:
                @pl.when(exists)
                def _():
                    direct(piece, at).start()
            else:
                @pl.when(gap)
                def _():
                    to_relay(piece, at, rising).start()

                @pl.when(jnp.logical_and(exists, jnp.logical_not(gap)))
                def _():
                    direct(piece, at).start()

    for piece in order[:4]:
        send_piece(piece)

    @pl.when(jnp.logical_not(has_down))
    def _():
        ext[pl.ds(0, halo), :] = jnp.zeros((halo, cols), F32)

    @pl.when(jnp.logical_not(has_up))
    def _():
        ext[pl.ds(halo + rows, halo), :] = jnp.zeros((halo, cols), F32)

    @pl.when(jnp.logical_not(has_left))
    def _():
        wide[:, pl.ds(0, halo)] = jnp.zeros((rows, halo), F32)

    @pl.when(jnp.logical_not(has_right))
    def _():
        wide[:, pl.ds(halo + cols, halo)] = jnp.zeros((rows, halo), F32)

    def clamped(lat):
        return jnp.clip(lat, 0, NLAT - 1)

    def courant_of(lat):
        inside = jnp.logical_and(lat >= 0, lat < NLAT)
        return jnp.where(inside, lat_ref[pl.ds(clamped(lat), 1), :], 0.0)

    for table in tables:
        table.wait()

    def prepare_row(i, carry):
        lat = first_row - 1 + i
        at = clamped(lat)
        row_rate[i] = jnp.broadcast_to(courant_of(lat), (NLON, NLON)).T
        row_sign[i] = jnp.broadcast_to(
            sign_ref[pl.ds(at, 1), :].astype(F32), (NLON, NLON)
        ).T
        high, low = split(sweep_matrix(at, lon_ref, zonal_ref, counts_ref).T)
        row_hi[i] = high
        row_lo[i] = low
        return carry

    lax.fori_loop(0, row_lats + 2, prepare_row, 0, unroll=3)

    for piece in order[4:]:
        send_piece(piece)

    def prepare_col(i, carry):
        at = clamped(first_col - 1 + i)
        high, low = split(sweep_matrix(at, lon_ref, zonal_ref, counts_ref))
        col_hi[i] = high
        col_lo[i] = low
        return carry

    def row_chunk(piece, start, width):
        at = pl.ds(start, width)

        @pl.when(has_down)
        def _():
            to_up(piece, at).wait_recv()

        @pl.when(has_up)
        def _():
            to_down(piece, at).wait_recv()

        def across(table):
            return jnp.concatenate([table] * (width // NLON), axis=1)

        for i in range(row_lats + 2):
            below = ext[pl.ds(i * NLON, NLON), at]
            center = ext[pl.ds((i + 1) * NLON, NLON), at]
            above = ext[pl.ds((i + 2) * NLON, NLON), at]
            moved = upwind(center, below, above, across(row_rate[i]), across(row_sign[i]) == 1.0)
            high, low = split(moved)
            row_mid[i, :, pl.ds(0, width)] = (
                dot(row_hi[i], high) + (dot(row_hi[i], low) + dot(row_lo[i], high))
            )
        mids = [row_mid[i, :, pl.ds(0, width)] for i in range(row_lats + 2)]
        own = pl.ds(pl.multiple_of(halo + start, NLON), width)
        for i in range(1, row_lats + 1):
            wide[pl.ds((i - 1) * NLON, NLON), own] = upwind(
                mids[i], mids[i - 1], mids[i + 1],
                across(row_rate[i]), across(row_sign[i]) == 1.0,
            )

    def lat_columns(index):
        return pl.ds(pl.multiple_of(index * NLON, NLON), NLON)

    def col_middle(i):
        lat = first_col - 1 + i
        from_below = sign_ref[pl.ds(clamped(lat), 1), :] == 1
        moved = upwind(
            wide[:, lat_columns(i + 1)], wide[:, lat_columns(i)], wide[:, lat_columns(i + 2)],
            courant_of(lat), from_below,
        )
        high, low = split(moved)
        col_mid[:, lat_columns(i)] = (
            dot(high, col_hi[i]) + (dot(low, col_hi[i]) + dot(high, col_lo[i]))
        )

    def col_final(k):
        lat = first_col + k
        from_below = sign_ref[pl.ds(lat, 1), :] == 1
        final[:, lat_columns(k)] = upwind(
            col_mid[:, lat_columns(k + 1)], col_mid[:, lat_columns(k)],
            col_mid[:, lat_columns(k + 2)], courant_of(lat), from_below,
        )

    core = lax.rem(r, 2)

    def half_rows(late):
        part = core if late else 1 - core
        return pl.ds(pl.multiple_of(part * (rows // 2), rows // 2), rows // 2)

    def to_left(lat, late):
        at = half_rows(late)
        return pltpu.make_async_remote_copy(
            wide.at[at, pl.ds(halo + lat * NLON, NLON)],
            wide.at[at, pl.ds(halo + cols + lat * NLON, NLON)],
            col_send.at[0, 2 * lat + late], col_recv.at[0, 2 * lat + late],
            device_id=left, device_id_type=MESH,
        )

    def to_right(lat, late):
        at = half_rows(late)
        return pltpu.make_async_remote_copy(
            wide.at[at, pl.ds(cols + lat * NLON, NLON)],
            wide.at[at, pl.ds(lat * NLON, NLON)],
            col_send.at[1, 2 * lat + late], col_recv.at[1, 2 * lat + late],
            device_id=right, device_id_type=MESH,
        )

    def edge_half(piece, late):
        start = (0, 1, col_lats - 2, col_lats - 1)[piece] * NLON
        at = pl.ds(start, NLON)

        @pl.when(jnp.logical_and(core == late, has_up))
        def _():
            to_down(piece, at).wait_recv()

        @pl.when(jnp.logical_and(core != late, has_down))
        def _():
            to_up(piece, at).wait_recv()

        def lat_rows(index):
            return pl.ds(pl.multiple_of(index * NLON, NLON), NLON)

        upper = 1 - core
        first = 4 - 4 * upper if late else 2 * upper
        for step in range(2 if late else 4):
            i = first + step
            moved = upwind(
                ext[lat_rows(i + 1), at], ext[lat_rows(i), at], ext[lat_rows(i + 2), at],
                row_rate[i], row_sign[i] == 1.0,
            )
            high, low = split(moved)
            edge_row_mid[piece, i] = (
                dot(row_hi[i], high) + (dot(row_hi[i], low) + dot(row_lo[i], high))
            )
        first = 2 - 2 * upper if late else 2 * upper
        for step in range(1, 3):
            i = first + step
            wide[lat_rows(i - 1), pl.ds(halo + start, NLON)] = upwind(
                edge_row_mid[piece, i], edge_row_mid[piece, i - 1], edge_row_mid[piece, i + 1],
                row_rate[i], row_sign[i] == 1.0,
            )
        if piece < 2:
            @pl.when(has_left)
            def _():
                to_left(piece, late).start()
        else:
            @pl.when(has_right)
            def _():
                to_right(piece - 2, late).start()

    def pass_on(piece):
        at = piece_columns(piece)
        for relay, rising in zip(RELAYS[piece], (True, False)):
            if relay is None:
                continue

            @pl.when(r == relay)
            def _():
                to_relay(piece, at, rising).wait_recv()
                from_relay(piece, at, rising).start()

    load.wait()
    for late in range(2):
        for piece in (0, 3, 1, 2):
            if late and piece in RELAYS:
                pass_on(piece)
            edge_half(piece, late)

    lax.fori_loop(0, col_lats + 2, prepare_col, 0, unroll=3)

    def interior(chunk, carry):
        for turn in sorted(set(RELAY_TURN.values())):
            @pl.when(chunk == turn)
            def _():
                for piece in RELAY_TURN:
                    if RELAY_TURN[piece] == turn:
                        pass_on(piece)

        row_chunk(4 + chunk, pl.multiple_of((chunk + 1) * WIDE, WIDE), WIDE)
        col_middle(2 * chunk + 2)
        col_middle(2 * chunk + 3)

        @pl.when(chunk > 0)
        def _():
            col_final(2 * chunk)
            col_final(2 * chunk + 1)

        return carry

    lax.fori_loop(0, inner, interior, 0)

    for i, lat in enumerate(EDGE_LATS):
        edge_rows[pl.ds(i, 1), :] = courant_of(first_col + lat)
        edge_rows[pl.ds(8 + i, 1), :] = sign_ref[
            pl.ds(clamped(first_col + lat), 1), :
        ].astype(F32)

    row_chunk(pieces - 2, inner_end, NLON)
    col_middle(col_lats - 4)
    col_final(col_lats - 6)
    row_chunk(pieces - 1, inner_end + NLON, NLON)
    for i in range(col_lats - 3, col_lats):
        col_middle(i)
    for k in range(col_lats - 5, col_lats - 2):
        col_final(k)

    @pl.when(has_right)
    def _():
        for lat in range(2):
            for late in range(2):
                to_left(lat, late).wait_recv()

    @pl.when(has_left)
    def _():
        for lat in range(2):
            for late in range(2):
                to_right(lat, late).wait_recv()

    for piece in order:
        at = piece_columns(piece)

        @pl.when(has_down)
        def _():
            to_down(piece, at).wait_send()

        @pl.when(has_up)
        def _():
            to_up(piece, at).wait_send()

        if piece in RELAYS:
            for relay, rising in zip(RELAYS[piece], (True, False)):
                if relay is None:
                    continue

                @pl.when(r == relay)
                def _():
                    from_relay(piece, at, rising).wait_send()

    for lat in range(2):
        for late in range(2):
            @pl.when(has_left)
            def _():
                to_left(lat, late).wait_send()

            @pl.when(has_right)
            def _():
                to_right(lat, late).wait_send()


def finish(
    final, wide, col_mid, col_hi, col_lo, edge_rows, out, edge_mid, edge_final, sems
):
    rows, cols = final.shape
    col_lats = cols // NLON
    edge = 2 * NLON
    inner = pl.ds(edge, cols - 2 * edge)
    stores = [pltpu.make_async_copy(final.at[:, inner], out.at[:, inner], sems.at[0])]
    stores[0].start()

    def lat_columns(index):
        return pl.ds(index * NLON, NLON)

    def row_of(lat):
        at = EDGE_LATS.index(lat)
        return edge_rows[pl.ds(at, 1), :], edge_rows[pl.ds(8 + at, 1), :] == 1.0

    def middle(lat):
        moved = upwind(
            wide[:, lat_columns(lat + 2)], wide[:, lat_columns(lat + 1)],
            wide[:, lat_columns(lat + 3)], *row_of(lat),
        )
        high, low = split(moved)
        i = lat + 1
        return dot(high, col_hi[i]) + (dot(low, col_hi[i]) + dot(high, col_lo[i]))

    for side, (outer, near) in enumerate((((-1, 0), (1, 2)), ((col_lats, col_lats - 1), (col_lats - 2, col_lats - 3)))):
        for at, lat in enumerate(outer):
            edge_mid[side, at] = middle(lat)
        mids = {lat: edge_mid[side, at] for at, lat in enumerate(outer)}
        mids |= {lat: col_mid[:, lat_columns(lat + 1)] for lat in near}
        first = 0 if side == 0 else cols - edge
        for lat in (outer[1], near[0]):
            place = lat * NLON - first
            edge_final[side, :, pl.ds(place, NLON)] = upwind(
                mids[lat], mids[lat - 1], mids[lat + 1], *row_of(lat)
            )
        store = pltpu.make_async_copy(
            edge_final.at[side], out.at[:, pl.ds(first, edge)], sems.at[1 + side]
        )
        store.start()
        stores.append(store)
    for store in stores:
        store.wait()


def solution(mesh):
    rows_n, cols_n = mesh.shape["row"], mesh.shape["col"]

    def per_device(covariance, lon_courant, lat_courant, zonal_upwind_sign, lat_sign, cycle_counts):
        rows, cols = covariance.shape
        row_lats, col_lats = rows // NLON, cols // NLON
        pieces = cols // WIDE + 3
        hbm = pl.BlockSpec(memory_space=pltpu.HBM)
        vmem = pl.BlockSpec(memory_space=pltpu.VMEM)
        parts = pl.pallas_call(
            functools.partial(kernel, rows_n, cols_n),
            out_shape=[
                jax.ShapeDtypeStruct((rows, cols), F32),
                jax.ShapeDtypeStruct((rows, cols + 4 * NLON), F32),
                jax.ShapeDtypeStruct((rows, cols + 2 * NLON), F32),
                jax.ShapeDtypeStruct((col_lats + 2, NLON, NLON), BF16),
                jax.ShapeDtypeStruct((col_lats + 2, NLON, NLON), BF16),
                jax.ShapeDtypeStruct((16, NLON), F32),
            ],
            in_specs=[hbm] * 6,
            out_specs=[vmem] * 6,
            scratch_shapes=[
                pltpu.VMEM((rows + 4 * NLON, cols), F32),
                pltpu.VMEM((2 * NLON, cols), F32),
                pltpu.VMEM((row_lats + 2, NLON, WIDE), F32),
                pltpu.VMEM((4, row_lats + 2, NLON, NLON), F32),
                pltpu.VMEM((NLAT, NLON), F32),
                pltpu.VMEM((NLAT, NLON), F32),
                pltpu.VMEM((NLAT, NLON), jnp.int32),
                pltpu.VMEM((NLAT, NLON), jnp.int32),
                pltpu.SMEM((NLAT,), jnp.int32),
                pltpu.VMEM((row_lats + 2, NLON, NLON), F32),
                pltpu.VMEM((row_lats + 2, NLON, NLON), F32),
                pltpu.VMEM((row_lats + 2, NLON, NLON), BF16),
                pltpu.VMEM((row_lats + 2, NLON, NLON), BF16),
                pltpu.SemaphoreType.DMA,
                pltpu.SemaphoreType.DMA((5,)),
                pltpu.SemaphoreType.DMA((2, pieces)),
                pltpu.SemaphoreType.DMA((2, pieces)),
                pltpu.SemaphoreType.DMA((pieces,)),
                pltpu.SemaphoreType.DMA((pieces,)),
                pltpu.SemaphoreType.DMA((2, 4)),
                pltpu.SemaphoreType.DMA((2, 4)),
            ],
            name="forecast",
            compiler_params=pltpu.CompilerParams(
                collective_id=0, has_side_effects=True, vmem_limit_bytes=36 * 2**20
            ),
        )(*[pltpu.with_memory_space_constraint(a, pltpu.HBM) for a in (covariance, lon_courant, lat_courant, zonal_upwind_sign, lat_sign, cycle_counts)])
        return pl.pallas_call(
            finish,
            out_shape=jax.ShapeDtypeStruct((rows, cols), F32),
            in_specs=[vmem] * 6,
            out_specs=hbm,
            scratch_shapes=[
                pltpu.VMEM((2, 2, rows, NLON), F32),
                pltpu.VMEM((2, rows, 2 * NLON), F32),
                pltpu.SemaphoreType.DMA((3,)),
            ],
            name="finish",
            compiler_params=pltpu.CompilerParams(vmem_limit_bytes=36 * 2**20),
        )(*parts)

    placed = (P("row", "col"), P(), P(), P(), P(), P())
    return jax.shard_map(
        per_device, mesh=mesh, in_specs=placed, out_specs=P("row", "col"), check_vma=False
    )
```
